128 devices in a mesh: row: 8 (over x_lo, z), col: 16 (over x_hi, y, core).
Axes of the slice: x: 4 (x_hi: 2, x_lo: 2; x = x_hi * 2 + x_lo), y: 4, z: 4, core: 2. Of those that a mesh axis runs over, the one named last changes fastest.
Arguments:
- amplitudes: float32 [16384, 16384], P('row', 'col'), may hold values from -1 to 1, as said below
- factors: float32 [16384, 256], P('row', 'col'), may hold values from -1.5 to 1.5
- occ_index: int32 [16384], replicated, may hold values from 0 to 63
- vir_index: int32 [16384], replicated, may hold values from 0 to 2047
- occ_energy: float32 [64], replicated, may hold values from -3 to -0.5
- vir_energy: float32 [2048], replicated, may hold values from 0.2 to 3
Outputs:
- new_amplitudes: float32 [16384, 16384], P('row', 'col')
The draws below stay inside these ranges and needn't reach their ends.
Inputs may be any that keep to these rules, and one draw needn't show every extreme that they name: amplitudes is symmetric: amplitudes[p, q] equals amplitudes[q, p].
All inputs are finite; a program needn't handle non-finite values.
Results may differ from the reference program's by a relative error of at most 0.000096.
Values sent between devices are 32-bit elements; how exact they have to be, the bound alone decides.
A program may use at most 64 MiB of HBM per device.

```python
import jax
import jax.numpy as jnp
from jax import lax

K = 256
NOCC = 64
NVIR = 2048
P_SIZE = 16384
N_ROW = 8


def draw_amplitudes(key, part):
    raw_normal = jnp.clip(jax.random.normal(key, (P_SIZE, P_SIZE), jnp.float32), -6.0, 6.0)
    symmetric = 0.5 * (raw_normal + raw_normal.T)
    return jnp.clip(symmetric / jnp.sqrt(jnp.float32(P_SIZE)), -1.0, 1.0)


def set_ends(array, stream_key, low, high):
    index_at = [jax.random.randint(jax.random.fold_in(stream_key, axis), (), 0, length) for axis, length in enumerate(array.shape)]
    widest = array.shape.index(max(array.shape))
    beside = index_at[:widest] + [(index_at[widest] + 1) % array.shape[widest]] + index_at[widest + 1:]
    return array.at[tuple(index_at)].set(low).at[tuple(beside)].set(high)


def shard_levels(key, extent, cuts, low, high):
    level, own = 1.0, jax.random.fold_in(key, 6)
    for position, parts in cuts:
        heights = jnp.exp(jax.random.uniform(jax.random.fold_in(own, position), (parts,), jnp.float32, low / len(cuts), high / len(cuts)))
        level = level * jnp.repeat(heights, extent[position] // parts).reshape([-1 if axis == position else 1 for axis in range(len(extent))])
    return level


def scatter_about(own_key, extent, spread, limit, shards=(), kind=jnp.bfloat16):
    entries = spread * jax.random.normal(own_key, extent, jnp.float32)
    if shards:
        entries = entries * shard_levels(own_key, extent, shards, -0.22, 0.18)
    return jnp.clip(entries, -limit, limit).astype(kind)


def setup_inputs(seed: int = 0) -> dict:
    seeds = jax.random.split(jax.random.key(seed), 7)
    amplitudes = draw_amplitudes(jax.random.fold_in(seeds[6], 71), 0)
    factors = scatter_about(seeds[1], (P_SIZE, K), 0.25, 1.5, ((0, 8), (1, 16)), jnp.float32)
    occ_index = set_ends(jax.random.randint(seeds[2], (P_SIZE,), 0, NOCC), jax.random.fold_in(seeds[2], 1), 0, NOCC - 1).astype(jnp.int32)
    vir_index = set_ends(jax.random.randint(seeds[3], (P_SIZE,), 0, NVIR), jax.random.fold_in(seeds[3], 1), 0, NVIR - 1).astype(jnp.int32)
    occ_energy = jnp.clip(jax.random.uniform(seeds[4], (NOCC,), jnp.float32, -3.0, -0.5), -3.0, -0.5)
    vir_energy = jnp.clip(jax.random.uniform(seeds[5], (NVIR,), jnp.float32, 0.2, 3.0), 0.2, 3.0)
    return dict(amplitudes=amplitudes, factors=factors, occ_index=occ_index, vir_index=vir_index, occ_energy=occ_energy, vir_energy=vir_energy)


def pair_energy(occ_index, vir_index, occ_energy, vir_energy):
    return vir_energy[vir_index] - occ_energy[occ_index]


def reference(amplitudes, factors, occ_index, vir_index, occ_energy, vir_energy):
    energy = pair_energy(occ_index, vir_index, occ_energy, vir_energy)
    product = jnp.dot(amplitudes, factors, precision=lax.Precision.HIGHEST, preferred_element_type=jnp.float32)
    dressed = factors + product
    row_blocks = dressed.reshape(N_ROW, P_SIZE // N_ROW, K)
    energy_blocks = energy.reshape(N_ROW, P_SIZE // N_ROW)

    def outer_block(items):
        row_block, row_energy = items
        contracted = lax.dot_general(row_block, dressed, (((1,), (1,)), ((), ())), precision=lax.Precision.HIGHEST, preferred_element_type=jnp.float32)
        return -contracted / (row_energy[:, None] + energy[None, :])

    stacked = lax.map(outer_block, (row_blocks, energy_blocks))
    return stacked.reshape(P_SIZE, P_SIZE)
```

```python
import functools

import jax
import jax.numpy as jnp
from jax import lax
from jax.experimental import pallas as pl
from jax.experimental.pallas import tpu as pltpu
from jax.sharding import PartitionSpec as P

MESH = pl.DeviceIdType.MESH
F32 = jnp.float32
BF16 = jnp.bfloat16
RING = ("pA", "mB", "pB", "mA", "fA", "fB")
NAMES = []
for t_ in range(2):
    for r_ in ("f0", "c0", "c1", "r0", "r1"):
        NAMES += [f"{r_}{t_}{m_}" for m_ in RING]
    NAMES += [f"s{q_}{j_}{t_}" for q_ in ("f", "r") for j_ in ("0", "m", "p", "2")]
    NAMES += [f"{m_}{t_}" for m_ in ("s1p", "s1m", "s2pA", "s2pB", "s2mA", "s2mB", "s3", "cx", "sw")]
    NAMES += [f"{m_}{t_}" for m_ in ("rxA", "rxB", "rrA", "rrB", "sr0x", "srmx", "srpx", "sr2x")]
NAMES += ["fxA", "fxB", "frA", "frB"]
ID = {n_: i_ for i_, n_ in enumerate(NAMES)}


def split(v):
    hi = v.astype(BF16)
    return hi, (v - hi.astype(F32)).astype(BF16)


def exchange_kernel(
    a_hbm, f_hbm, dr_hbm, dc_hbm,
    abuf, ah, al, ft, fhl, rlp, rlm, pt, r1a, r1b, r2p, r2m, sx, r3, dc, dn, dr, qlp, qlm,
    ssem, rsem, asem, lsem,
):
    row, col = lax.axis_index("row"), lax.axis_index("col")
    x_lo, z = row // 4, row % 4
    s = col // 2
    x_hi, y, core = s // 4, s % 4, col % 2
    x = 2 * x_hi + x_lo

    def dev(xh, xl, yy, zz, cc):
        return (xl * 4 + zz, xh * 8 + yy * 2 + cc)

    yp, ym, y2 = (y + 1) % 4, (y + 3) % 4, (y + 2) % 4
    zp, zm, z2 = (z + 1) % 4, (z + 3) % 4, (z + 2) % 4
    xp, xm = (x + 1) % 4, (x + 3) % 4
    d_yp, d_ym = dev(x_hi, x_lo, yp, z, core), dev(x_hi, x_lo, ym, z, core)
    d_zp, d_zm = dev(x_hi, x_lo, y, zp, core), dev(x_hi, x_lo, y, zm, core)
    d_xp, d_xm = dev(xp // 2, xp % 2, y, z, core), dev(xm // 2, xm % 2, y, z, core)
    d_xn = dev(x_hi, 1 - x_lo, y, z, core)
    d_sib = dev(x_hi, x_lo, y, z, 1 - core)
    d_tr = dev(x_lo, x_hi, z, y, core)
    diag = row == s
    off_diag = row != s

    sends = {}

    def make(name, src, dst, to):
        i = ID[name]
        return pltpu.make_async_remote_copy(
            src_ref=src, dst_ref=dst, send_sem=ssem.at[i], recv_sem=rsem.at[i],
            device_id=to, device_id_type=MESH)

    def start(name, src, dst, to):
        sends[name] = make(name, src, dst, to)
        sends[name].start()

    def recv(name, ref):
        make(name, ref, ref, d_sib).wait_recv()

    class Ring:
        def __init__(self, name, slot, pos, up, down, half):
            self.n, self.slot, self.up, self.down, self.half = name, slot, up, down, half
            self.p, self.u, self.d, self.o = pos, (pos + 1) % 4, (pos + 3) % 4, (pos + 2) % 4

        def part(self, ref, which):
            return ref.at[pl.ds(which * self.half, self.half)]

        def own(self, src=None):
            dst = self.slot(self.p)
            src = dst if src is None else src
            for m, w, to in (("pA", 0, self.up), ("mB", 1, self.down), ("pB", 1, self.up), ("mA", 0, self.down)):
                start(self.n + m, self.part(src, w), self.part(dst, w), to)

        def fwd(self):
            ref = self.part(self.slot(self.d), 0)
            recv(self.n + "pA", ref)
            start(self.n + "fA", ref, ref, self.up)
            ref = self.part(self.slot(self.u), 1)
            recv(self.n + "mB", ref)
            start(self.n + "fB", ref, ref, self.down)

        def near(self):
            recv(self.n + "pB", self.part(self.slot(self.d), 1))
            recv(self.n + "mA", self.part(self.slot(self.u), 0))

        def far(self):
            recv(self.n + "fA", self.part(self.slot(self.o), 0))
            recv(self.n + "fB", self.part(self.slot(self.o), 1))

    def a_copy(i):
        rows = pl.ds(i * 256, 256)
        return pltpu.make_async_copy(a_hbm.at[rows], abuf.at[rows], asem.at[i])

    for i in range(8):
        a_copy(i).start()
    own_f = pltpu.make_async_copy(f_hbm, ft.at[x_hi, y, core], lsem.at[0])
    own_f.start()

    barrier = pltpu.get_barrier_semaphore()
    for d in (d_yp, d_ym, d_zp, d_zm, d_xp, d_xm, d_sib):
        pl.semaphore_signal(barrier, inc=1, device_id=d, device_id_type=MESH)

    @pl.when(off_diag)
    def _():
        pl.semaphore_signal(barrier, inc=1, device_id=d_tr, device_id_type=MESH)
        pl.semaphore_wait(barrier, 8)

    @pl.when(diag)
    def _():
        pl.semaphore_wait(barrier, 7)

    def f_slot(h):
        return lambda i: ft.at[h, i, core]

    fr = [Ring(f"f0{t}", f_slot(x_hi if t == 0 else 1 - x_hi), y, d_yp, d_ym, 8) for t in range(2)]
    lo8, hi8 = pl.ds(0, 8), pl.ds(8, 8)
    start("fxA", f_hbm.at[lo8], rlp, d_xp)
    start("fxB", f_hbm.at[hi8], rlm, d_xm)
    fr[0].own(f_hbm)
    sib_f0 = ft.at[x_hi, y, core]
    start("sf00", f_hbm, sib_f0, d_sib)

    def split_a(lo, hi):
        def body(i, carry):
            a_copy(i).wait()
            rows = pl.ds(pl.multiple_of(i * 256, 256), 256)
            for xl in range(2):
                for zz in range(4):
                    r = xl * 4 + zz
                    h, l = split(abuf[rows, r * 128:(r + 1) * 128])
                    ah[zz, rows, xl * 128:(xl + 1) * 128] = h
                    al[zz, rows, xl * 128:(xl + 1) * 128] = l
            return carry
        lax.fori_loop(lo, hi, body, 0)

    def f_sib(t, j, pos):
        h = x_hi if t == 0 else 1 - x_hi
        start(f"sf{j}{t}", ft.at[h, pos, core], ft.at[h, pos, core], d_sib)

    def f_sib_recv(t):
        h = x_hi if t == 0 else 1 - x_hi
        for j, pos in (("0", y), ("m", ym), ("p", yp), ("2", y2)):
            recv(f"sf{j}{t}", ft.at[h, pos, 1 - core])

    split_a(0, 4)
    recv("fxA", rlp)
    start("frA", rlp, ft.at[1 - xp // 2, y, core, lo8], d_xp)
    recv("fxB", rlm)
    start("frB", rlm, ft.at[1 - xm // 2, y, core, hi8], d_xm)
    split_a(4, 6)
    fr[0].fwd()
    fr[0].near()
    f_sib(0, "m", ym)
    f_sib(0, "p", yp)
    split_a(6, 8)
    recv("frA", ft.at[1 - x_hi, y, core, lo8])
    recv("frB", ft.at[1 - x_hi, y, core, hi8])
    fr[1].own()
    f_sib(1, "0", y)
    fr[0].far()
    f_sib(0, "2", y2)
    own_f.wait()
    f_sib_recv(0)

    def split_f(t):
        h = x_hi if t == 0 else 1 - x_hi
        hi, lo = split(ft[h].reshape(128, 2048))
        fhl[0:128] = hi
        fhl[128:256] = lo

    def product(t, zz):
        h = x_hi if t == 0 else 1 - x_hi
        both = jnp.dot(fhl[...], ah[zz], preferred_element_type=F32)
        low = jnp.dot(fhl[0:128], al[zz], preferred_element_type=F32)
        p = both[:128] + (both[128:] + low)
        for xl in range(2):
            pt[t, zz, xl] = p[:, xl * 128:(xl + 1) * 128]

        @pl.when(diag)
        def _():
            for xl in range(2):
                at = pl.multiple_of(core * 1024 + (xl * 4 + zz) * 128, 128)
                pt[t, zz, xl] += ft[h, :, :, :, pl.ds(at, 128)].reshape(128, 128)

    up, dn_ = pl.ds(0, 64), pl.ds(64, 64)

    def reduce_first(t):
        start(f"s1p{t}", pt.at[t, z2, :, up], r1a.at[t], d_zp)
        start(f"s1m{t}", pt.at[t, z2, :, dn_], r1b.at[t], d_zm)

    def reduce_near(t, j):
        if j == "p":
            start(f"s2pB{t}", pt.at[t, zp, :, dn_], r2p.at[t, :, dn_], d_zp)
        else:
            start(f"s2mA{t}", pt.at[t, zm, :, up], r2m.at[t, :, up], d_zm)

    def reduce_relay(t):
        recv(f"s1p{t}", r1a.at[t])
        pt[t, zp, :, 0:64] += r1a[t]
        start(f"s2pA{t}", pt.at[t, zp, :, up], r2p.at[t, :, up], d_zp)
        recv(f"s1m{t}", r1b.at[t])
        pt[t, zm, :, 64:128] += r1b[t]
        start(f"s2mB{t}", pt.at[t, zm, :, dn_], r2m.at[t, :, dn_], d_zm)

    def reduce_cross(t):
        recv(f"s2pB{t}", r2p.at[t, :, dn_])
        recv(f"s2mA{t}", r2m.at[t, :, up])
        recv(f"s2pA{t}", r2p.at[t, :, up])
        recv(f"s2mB{t}", r2m.at[t, :, dn_])
        o = 1 - x_lo
        sx[t] = pt[t, z, o] + r2p[t, o] + r2m[t, o]
        start(f"s3{t}", sx.at[t], r3.at[t], d_xn)

    def kc(t):
        return x_hi if t == 0 else 1 - x_hi

    def kr(t):
        return x_lo if t == 0 else 1 - x_lo

    def c_ring(t, j):
        xl = x_lo if j == 0 else 1 - x_lo
        return Ring(f"c{j}{t}", lambda i: dc.at[kc(t), xl * 4 + i], z, d_zp, d_zm, 64)

    def r_ring(t, j):
        xh = x_hi if j == 0 else 1 - x_hi
        return Ring(f"r{j}{t}", lambda i: dr.at[kr(t), core, xh * 4 + i], y, d_yp, d_ym, 64)

    cr = [[c_ring(t, j) for j in range(2)] for t in range(2)]
    rr = [[r_ring(t, j) for j in range(2)] for t in range(2)]

    def dressed(t):
        own = pt[t, z, x_lo] + r2p[t, x_lo] + r2m[t, x_lo]
        recv(f"s3{t}", r3.at[t])
        d = own + r3[t]
        dc[kc(t), row] = d
        dt = d.T

        @pl.when(off_diag)
        def _():
            dn[t] = dt
            make(f"sw{t}", dn.at[t], dr.at[kc(t), core, row], d_tr).start()

        @pl.when(diag)
        def _():
            dr[kc(t), core, row] = dt

        start(f"cx{t}", dc.at[kc(t), row], dc.at[kc(t), row], d_xn)
        cr[t][0].own()

    def swap_in(t):
        @pl.when(off_diag)
        def _():
            recv(f"sw{t}", dr.at[kr(t), core, s])

        mine = dr.at[kr(t), core, s]
        start(f"rxA{t}", mine.at[up], qlp.at[t], d_xp)
        start(f"rxB{t}", mine.at[dn_], qlm.at[t], d_xm)
        rr[t][0].own()
        start(f"sr0{t}", mine, mine, d_sib)

    def c_other(t):
        recv(f"cx{t}", dc.at[kc(t), (1 - x_lo) * 4 + z])
        cr[t][1].own()

    def r_relay(t):
        k = 1 - kr(t)
        recv(f"rxA{t}", qlp.at[t])
        start(f"rrA{t}", qlp.at[t], dr.at[k, core, (1 - xp // 2) * 4 + y, up], d_xp)
        recv(f"rxB{t}", qlm.at[t])
        start(f"rrB{t}", qlm.at[t], dr.at[k, core, (1 - xm // 2) * 4 + y, dn_], d_xm)

    def r_sib(t, j, tag, pos):
        xh = x_hi if j == 0 else 1 - x_hi
        ref = dr.at[kr(t), core, xh * 4 + pos]
        start(f"sr{tag}{t}" if j == 0 else f"sr{tag}x{t}", ref, ref, d_sib)

    def r_other(t):
        o = (1 - x_hi) * 4 + y
        recv(f"rrA{t}", dr.at[kr(t), core, o, up])
        recv(f"rrB{t}", dr.at[kr(t), core, o, dn_])
        rr[t][1].own()
        r_sib(t, 1, "0", y)

    def r_near(t, j):
        rr[t][j].near()
        r_sib(t, j, "m", ym)
        r_sib(t, j, "p", yp)

    def r_far(t, j):
        rr[t][j].far()
        r_sib(t, j, "2", y2)

    def r_sib_recv(t):
        for j in range(2):
            xh = x_hi if j == 0 else 1 - x_hi
            for tag, pos in (("0", y), ("m", ym), ("p", yp), ("2", y2)):
                recv(f"sr{tag}{t}" if j == 0 else f"sr{tag}x{t}", dr.at[kr(t), 1 - core, xh * 4 + pos])

    split_f(0)
    product(0, z2)
    reduce_first(0)
    product(0, zp)
    reduce_near(0, "p")
    product(0, zm)
    reduce_near(0, "m")
    fr[1].fwd()
    fr[1].near()
    f_sib(1, "m", ym)
    f_sib(1, "p", yp)
    reduce_relay(0)
    product(0, z)
    fr[1].far()
    f_sib(1, "2", y2)
    reduce_cross(0)
    f_sib_recv(1)
    split_f(1)
    product(1, z2)
    reduce_first(1)
    dressed(0)
    product(1, zp)
    reduce_near(1, "p")
    product(1, zm)
    reduce_near(1, "m")
    swap_in(0)
    reduce_relay(1)
    product(1, z)
    r_relay(0)
    c_other(0)
    cr[0][0].fwd()
    rr[0][0].fwd()
    r_other(0)
    r_near(0, 0)
    reduce_cross(1)
    cr[0][1].fwd()
    rr[0][1].fwd()
    dressed(1)
    cr[0][0].near()
    r_far(0, 0)
    r_near(0, 1)
    cr[0][0].far()
    cr[0][1].near()
    r_far(0, 1)
    cr[0][1].far()
    swap_in(1)
    r_sib_recv(0)
    outs = [
        pltpu.make_async_copy(dr.at[kr(0)], dr_hbm.at[kr(0)], lsem.at[1]),
        pltpu.make_async_copy(dc.at[kc(0)], dc_hbm.at[kc(0)], lsem.at[2]),
    ]
    for o in outs:
        o.start()
    c_other(1)
    r_relay(1)
    cr[1][0].fwd()
    rr[1][0].fwd()
    r_other(1)
    r_near(1, 0)
    cr[1][1].fwd()
    rr[1][1].fwd()
    cr[1][0].near()
    cr[1][0].far()
    r_far(1, 0)
    r_near(1, 1)
    cr[1][1].near()
    cr[1][1].far()
    last = pltpu.make_async_copy(dc.at[kc(1)], dc_hbm.at[kc(1)], lsem.at[3])
    last.start()
    r_far(1, 1)
    r_sib_recv(1)
    final = pltpu.make_async_copy(dr.at[kr(1)], dr_hbm.at[kr(1)], lsem.at[4])
    final.start()
    for c in sends.values():
        c.wait_send()

    @pl.when(off_diag)
    def _():
        for t in range(2):
            make(f"sw{t}", dn.at[t], dr.at[kc(t), core, row], d_tr).wait_send()

    for o in outs + [last, final]:
        o.wait()


def outer_kernel(dr_ref, dc_ref, occ_ref, vir_ref, eocc_ref, evir_ref, out_ref, ch, cl, ecol, erow):
    @pl.when(pl.program_id(0) == 0)
    def _():
        for k in range(2):
            for r in range(8):
                h, l = split(dc_ref[k, r])
                ch[k * 128:(k + 1) * 128, r * 128:(r + 1) * 128] = h
                cl[k * 128:(k + 1) * 128, r * 128:(r + 1) * 128] = l
        row, col = lax.axis_index("row"), lax.axis_index("col")
        occ_rows, vir_rows = [], []
        for start, size in ((row * 16, 16), (col * 8, 8)):
            at = pl.ds(pl.multiple_of(start, 8), size)
            occ_rows.append(occ_ref[at])
            vir_rows.append(vir_ref[at])
        occ = jnp.concatenate(occ_rows, axis=0)
        vir = jnp.concatenate(vir_rows, axis=0)
        low, high = vir & 127, vir >> 7
        picked = jnp.zeros((24, 128), F32)
        for h in range(16):
            table = jnp.broadcast_to(evir_ref[h:h + 1], (24, 128))
            got = jnp.take_along_axis(table, low, axis=1, mode="promise_in_bounds")
            picked = jnp.where(high == h, got, picked)
        taken = jnp.zeros((24, 128), F32)
        for o in range(64):
            taken = jnp.where(occ == o, eocc_ref[o], taken)
        negative = taken - picked
        erow[...] = negative[16:24]
        for i in range(16):
            ecol[i * 128:(i + 1) * 128] = jnp.broadcast_to(negative[i:i + 1], (128, 128)).T

    x = jnp.concatenate([dr_ref[0], dr_ref[1]], axis=1)
    h, l = split(x)
    acc = jnp.dot(h, ch[...], preferred_element_type=F32)
    acc += jnp.dot(l, ch[...], preferred_element_type=F32)
    acc += jnp.dot(h, cl[...], preferred_element_type=F32)
    rows = pl.ds(pl.multiple_of(pl.program_id(0) * 256, 256), 256)
    e = ecol[rows]
    for n in range(8):
        lanes = slice(n * 128, (n + 1) * 128)
        out_ref[:, lanes] = acc[:, lanes] / (e + erow[n:n + 1])


def local(amplitudes, factors, occ_index, vir_index, occ_energy, vir_energy):
    hbm = pl.BlockSpec(memory_space=pl.ANY)
    vmem = lambda *shape: pltpu.VMEM(shape, F32)
    dr, dc = pl.pallas_call(
        exchange_kernel,
        out_shape=(
            jax.ShapeDtypeStruct((2, 2, 8, 128, 128), F32),
            jax.ShapeDtypeStruct((2, 8, 128, 128), F32),
        ),
        in_specs=[hbm, hbm],
        out_specs=(hbm, hbm),
        scratch_shapes=[
            vmem(2048, 1024),
            pltpu.VMEM((4, 2048, 256), BF16),
            pltpu.VMEM((4, 2048, 256), BF16),
            vmem(2, 4, 2, 16, 2048),
            pltpu.VMEM((256, 2048), BF16),
            vmem(8, 2048),
            vmem(8, 2048),
            vmem(2, 4, 2, 128, 128),
            vmem(2, 2, 64, 128),
            vmem(2, 2, 64, 128),
            vmem(2, 2, 128, 128),
            vmem(2, 2, 128, 128),
            vmem(2, 128, 128),
            vmem(2, 128, 128),
            vmem(2, 8, 128, 128),
            vmem(2, 128, 128),
            vmem(2, 2, 8, 128, 128),
            vmem(2, 64, 128),
            vmem(2, 64, 128),
            pltpu.SemaphoreType.DMA((len(NAMES),)),
            pltpu.SemaphoreType.DMA((len(NAMES),)),
            pltpu.SemaphoreType.DMA((8,)),
            pltpu.SemaphoreType.DMA((5,)),
        ],
        compiler_params=pltpu.CompilerParams(
            collective_id=0, has_side_effects=True, vmem_limit_bytes=48 * 1024 * 1024),
        name="exchange",
    )(amplitudes, factors.T)
    whole = lambda *shape: pl.BlockSpec(shape, lambda i: (0,) * len(shape))
    return pl.pallas_call(
        outer_kernel,
        grid=(8,),
        out_shape=jax.ShapeDtypeStruct((2048, 1024), F32),
        in_specs=[
            pl.BlockSpec((2, 256, 128), lambda i: (0, i, 0)),
            whole(2, 8, 128, 128),
            whole(128, 128),
            whole(128, 128),
            pl.BlockSpec(memory_space=pltpu.SMEM),
            whole(16, 128),
        ],
        out_specs=pl.BlockSpec((256, 1024), lambda i: (i, 0)),
        scratch_shapes=[
            pltpu.VMEM((256, 1024), BF16),
            pltpu.VMEM((256, 1024), BF16),
            vmem(2048, 128),
            vmem(8, 128),
        ],
        compiler_params=pltpu.CompilerParams(vmem_limit_bytes=32 * 1024 * 1024),
        name="outer",
    )(
        dr.reshape(2, 2048, 128), dc, occ_index.reshape(128, 128), vir_index.reshape(128, 128),
        occ_energy, vir_energy.reshape(16, 128),
    )


def solution(mesh):
    return jax.shard_map(
        local,
        mesh=mesh,
        in_specs=(P("row", "col"), P("row", "col"), P(), P(), P(), P()),
        out_specs=P("row", "col"),
        check_vma=False,
    )
```

```python
import functools

import jax
import jax.numpy as jnp
from jax import lax
from jax.experimental import pallas as pl
from jax.experimental.pallas import tpu as pltpu
from jax.sharding import PartitionSpec as P

MESH = pl.DeviceIdType.MESH
F32 = jnp.float32
BF16 = jnp.bfloat16
RING = ("pA", "mB", "pB", "mA", "fA", "fB")
NAMES = ["fx"]
for t_ in range(2):
    for r_ in ("f0", "f1"):
        NAMES += [f"{r_}{m_}" for m_ in RING if t_ == 0]
    for r_ in ("c0", "c1", "r0", "r1"):
        NAMES += [f"{r_}{t_}{m_}" for m_ in RING]
    NAMES += [f"{q_}{t_}{j_}" for q_ in ("sf", "sr", "sq") for j_ in ("0", "m", "p", "2")]
    NAMES += [f"{m_}{t_}" for m_ in ("s1p", "s1m", "s2pA", "s2pB", "s2mA", "s2mB", "s3", "cx", "sw", "sx")]
ID = {n_: i_ for i_, n_ in enumerate(NAMES)}

ORDER = (
    "f0.own", "spA0", "spA1", "spA2", "spA3", "f0.fA", "f0.fB", "f0.nm", "f0.np", "f1.own", "f0.far", "spF0",
    "mm0.2", "mm0.p", "f1.fA", "f1.fB", "mm0.m", "mm0.0", "f1.nm", "f1.np", "rl0p", "rl0m", "f1.far", "spF1",
    "mm1.2", "mm1.p", "mm1.m", "mm1.0", "cr0", "rl1p", "rl1m", "c00.own", "cr1", "c00.fA", "c10.own", "c00.fB",
    "c00.nm", "c00.np", "r00.own", "c01.own", "r10.own", "c10.fB", "c10.fA", "c10.np", "r00.fA", "r00.fB",
    "c10.nm", "c00.far", "r00.nm", "r00.np", "c11.own", "c01.fA", "c01.fB", "r10.fA", "r10.fB", "c01.nm",
    "c01.np", "r10.nm", "r10.np", "c10.far", "r01.own", "r00.far", "c11.fA", "c11.fB", "r11.own", "c11.nm",
    "c11.np", "r10.far", "c01.far", "rf0", "r01.fA", "r01.fB", "c11.far", "r01.nm", "r01.np", "r11.fA",
    "r11.fB", "r11.nm", "r11.np", "r01.far", "r11.far", "rf1",
)


def split(v):
    hi = v.astype(BF16)
    return hi, (v - hi.astype(F32)).astype(BF16)


def exchange_kernel(
    a_hbm, f_hbm, dr, dc,
    abuf, ah, al, ft, fhl, pt, r1a, r1b, r2p, r2m, sx, r3, dp, dn,
    ssem, rsem, asem, lsem, msem,
):
    row, col = lax.axis_index("row"), lax.axis_index("col")
    x_lo, z = row // 4, row % 4
    s = col // 2
    x_hi, y, core = s // 4, s % 4, col % 2

    def dev(xh, xl, yy, zz, cc):
        return (xl * 4 + zz, xh * 8 + yy * 2 + cc)

    yp, ym, y2 = (y + 1) % 4, (y + 3) % 4, (y + 2) % 4
    zp, zm, z2 = (z + 1) % 4, (z + 3) % 4, (z + 2) % 4
    d_yp, d_ym = dev(x_hi, x_lo, yp, z, core), dev(x_hi, x_lo, ym, z, core)
    d_zp, d_zm = dev(x_hi, x_lo, y, zp, core), dev(x_hi, x_lo, y, zm, core)
    d_x2 = dev(1 - x_hi, x_lo, y, z, core)
    d_xn = dev(x_hi, 1 - x_lo, y, z, core)
    d_sib = dev(x_hi, x_lo, y, z, 1 - core)
    d_tr = dev(x_lo, x_hi, z, y, core)
    d_tx = dev(1 - x_lo, x_hi, z, y, core)
    d_from_tx = dev(x_lo, 1 - x_hi, z, y, core)
    diag = row == s
    off_diag = row != s

    sends, got = {}, set()

    def make(name, src, dst, to):
        i = ID[name]
        return pltpu.make_async_remote_copy(
            src_ref=src, dst_ref=dst, send_sem=ssem.at[i], recv_sem=rsem.at[i],
            device_id=to, device_id_type=MESH)

    def start(name, src, dst, to):
        sends[name] = make(name, src, dst, to)
        sends[name].start()

    def recv(name, ref):
        if name not in got:
            got.add(name)
            make(name, ref, ref, d_sib).wait_recv()

    steps = {}

    def step(name):
        def keep(f):
            steps[name] = f
        return keep

    def ring(n, slot, pos, to_up, to_down, half, own, sib=None):
        u, d, o = (pos + 1) % 4, (pos + 3) % 4, (pos + 2) % 4

        def part(i, which):
            return slot(i).at[pl.ds(which * half, half)]

        def to_sib(tag, i):
            if sib is not None:
                start(sib + tag, slot(i), slot(i), d_sib)

        def send_own(src=None):
            src = slot(pos) if src is None else src
            for m, w, to in (("pA", 0, to_up), ("mB", 1, to_down), ("pB", 1, to_up), ("mA", 0, to_down)):
                start(n + m, src.at[pl.ds(w * half, half)], part(pos, w), to)
            if sib is not None:
                start(sib + "0", src, slot(pos), d_sib)

        @step(n + ".own")
        def _():
            own(send_own)

        @step(n + ".fA")
        def _():
            recv(n + "pA", part(d, 0))
            start(n + "fA", part(d, 0), part(d, 0), to_up)

        @step(n + ".fB")
        def _():
            recv(n + "mB", part(u, 1))
            start(n + "fB", part(u, 1), part(u, 1), to_down)

        @step(n + ".nm")
        def _():
            recv(n + "pA", part(d, 0))
            recv(n + "pB", part(d, 1))
            to_sib("m", d)

        @step(n + ".np")
        def _():
            recv(n + "mA", part(u, 0))
            recv(n + "mB", part(u, 1))
            to_sib("p", u)

        @step(n + ".far")
        def _():
            recv(n + "fA", part(o, 0))
            recv(n + "fB", part(o, 1))
            to_sib("2", o)

    def a_copy(i):
        rows = pl.ds(i * 256, 256)
        return pltpu.make_async_copy(a_hbm.at[rows], abuf.at[rows], asem.at[i])

    for i in range(8):
        a_copy(i).start()
    own_f = pltpu.make_async_copy(f_hbm, ft.at[x_hi, y, core], lsem.at[0])
    own_f.start()

    barrier = pltpu.get_barrier_semaphore()
    for d in (d_yp, d_ym, d_zp, d_zm, d_x2, d_xn, d_sib, d_from_tx):
        pl.semaphore_signal(barrier, inc=1, device_id=d, device_id_type=MESH)

    @pl.when(off_diag)
    def _():
        pl.semaphore_signal(barrier, inc=1, device_id=d_tr, device_id_type=MESH)
        pl.semaphore_wait(barrier, 9)

    @pl.when(diag)
    def _():
        pl.semaphore_wait(barrier, 8)

    def kf(t):
        return x_hi if t == 0 else 1 - x_hi

    def kr(t):
        return x_lo if t == 0 else 1 - x_lo

    def own_f0(send):
        start("fx", f_hbm, ft.at[x_hi, y, core], d_x2)
        send(f_hbm)

    def own_f1(send):
        recv("fx", ft.at[1 - x_hi, y, core])
        send()

    for t, own in enumerate((own_f0, own_f1)):
        ring(f"f{t}", lambda i, t=t: ft.at[kf(t), i, core], y, d_yp, d_ym, 8, own, f"sf{t}")

    for q in range(4):
        @step(f"spA{q}")
        def _(q=q):
            def body(i, carry):
                a_copy(i).wait()
                rows = pl.ds(pl.multiple_of(i * 256, 256), 256)
                for xl in range(2):
                    for zz in range(4):
                        r = xl * 4 + zz
                        h, l = split(abuf[rows, r * 128:(r + 1) * 128])
                        ah[zz, rows, xl * 128:(xl + 1) * 128] = h
                        al[zz, rows, xl * 128:(xl + 1) * 128] = l
                return carry
            lax.fori_loop(2 * q, 2 * q + 2, body, 0)

    up, down = pl.ds(0, 64), pl.ds(64, 64)

    def product(t, zz):
        h = kf(t)
        both = jnp.dot(fhl[...], ah[zz], preferred_element_type=F32)
        low = jnp.dot(fhl[0:128], al[zz], preferred_element_type=F32)
        p = both[:128] + (both[128:] + low)
        for xl in range(2):
            pt[t, zz, xl] = p[:, xl * 128:(xl + 1) * 128]

        @pl.when(diag)
        def _():
            for xl in range(2):
                at = pl.multiple_of(core * 1024 + (xl * 4 + zz) * 128, 128)
                pt[t, zz, xl] += ft[h, :, :, :, pl.ds(at, 128)].reshape(128, 128)

    for t in range(2):
        @step(f"spF{t}")
        def _(t=t):
            if t == 0:
                own_f.wait()
            for j, pos in (("0", y), ("m", ym), ("p", yp), ("2", y2)):
                recv(f"sf{t}{j}", ft.at[kf(t), pos, 1 - core])
            hi, lo = split(ft[kf(t)].reshape(128, 2048))
            fhl[0:128] = hi
            fhl[128:256] = lo

        @step(f"mm{t}.2")
        def _(t=t):
            product(t, z2)
            start(f"s1p{t}", pt.at[t, z2, :, up], r1a.at[t], d_zp)
            start(f"s1m{t}", pt.at[t, z2, :, down], r1b.at[t], d_zm)

        @step(f"mm{t}.p")
        def _(t=t):
            product(t, zp)
            start(f"s2pB{t}", pt.at[t, zp, :, down], r2p.at[t, :, down], d_zp)

        @step(f"mm{t}.m")
        def _(t=t):
            product(t, zm)
            start(f"s2mA{t}", pt.at[t, zm, :, up], r2m.at[t, :, up], d_zm)

        @step(f"mm{t}.0")
        def _(t=t):
            product(t, z)

        @step(f"rl{t}p")
        def _(t=t):
            recv(f"s1p{t}", r1a.at[t])
            pt[t, zp, :, 0:64] += r1a[t]
            start(f"s2pA{t}", pt.at[t, zp, :, up], r2p.at[t, :, up], d_zp)

        @step(f"rl{t}m")
        def _(t=t):
            recv(f"s1m{t}", r1b.at[t])
            pt[t, zm, :, 64:128] += r1b[t]
            start(f"s2mB{t}", pt.at[t, zm, :, down], r2m.at[t, :, down], d_zm)

        @step(f"cr{t}")
        def _(t=t):
            recv(f"s2pA{t}", r2p.at[t, :, up])
            recv(f"s2pB{t}", r2p.at[t, :, down])
            recv(f"s2mA{t}", r2m.at[t, :, up])
            recv(f"s2mB{t}", r2m.at[t, :, down])
            o = 1 - x_lo
            sx[t] = pt[t, z, o] + r2p[t, o] + r2m[t, o]
            start(f"s3{t}", sx.at[t], r3.at[t], d_xn)

        def own_c0(send, t=t):
            own = pt[t, z, x_lo] + r2p[t, x_lo] + r2m[t, x_lo]
            recv(f"s3{t}", r3.at[t])
            d = own + r3[t]
            dn[t] = d.T
            start(f"sx{t}", dn.at[t], dr.at[kf(t), core, row], d_tx)

            @pl.when(off_diag)
            def _():
                make(f"sw{t}", dn.at[t], dr.at[kf(t), core, row], d_tr).start()

            @pl.when(diag)
            def _():
                pltpu.make_async_copy(dn.at[t], dr.at[kf(t), core, row], msem.at[t]).start()

            dp[t] = d
            start(f"cx{t}", dp.at[t], dc.at[kf(t), row], d_xn)
            send(dp.at[t])
            pltpu.make_async_copy(dp.at[t], dc.at[kf(t), row], lsem.at[1 + t]).start()

        def own_c1(send, t=t):
            recv(f"cx{t}", dc.at[kf(t), (1 - x_lo) * 4 + z])
            send()

        def own_r0(send, t=t):
            mine = dr.at[kr(t), core, s]

            @pl.when(off_diag)
            def _():
                make(f"sw{t}", mine, mine, d_sib).wait_recv()

            @pl.when(diag)
            def _():
                pltpu.make_async_copy(dn.at[t], mine, msem.at[t]).wait()

            send()

        def own_r1(send, t=t):
            recv(f"sx{t}", dr.at[kr(t), core, (1 - x_hi) * 4 + y])
            send()

        for j, own in enumerate((own_c0, own_c1)):
            xl = x_lo if j == 0 else 1 - x_lo
            ring(f"c{j}{t}", lambda i, t=t, xl=xl: dc.at[kf(t), xl * 4 + i], z, d_zp, d_zm, 64, own)
        for j, own in enumerate((own_r0, own_r1)):
            xh = x_hi if j == 0 else 1 - x_hi
            ring(f"r{j}{t}", lambda i, t=t, xh=xh: dr.at[kr(t), core, xh * 4 + i], y, d_yp, d_ym, 64, own,
                 f"{'sr' if j == 0 else 'sq'}{t}")

        @step(f"rf{t}")
        def _(t=t):
            for j in range(2):
                xh = x_hi if j == 0 else 1 - x_hi
                for tag, pos in (("0", y), ("m", ym), ("p", yp), ("2", y2)):
                    recv(f"{'sr' if j == 0 else 'sq'}{t}{tag}", dr.at[kr(t), 1 - core, xh * 4 + pos])

    for name in ORDER:
        steps[name]()

    for c in sends.values():
        c.wait_send()

    @pl.when(off_diag)
    def _():
        for t in range(2):
            make(f"sw{t}", dn.at[t], dr.at[kf(t), core, row], d_tr).wait_send()

    for t in range(2):
        pltpu.make_async_copy(dp.at[t], dc.at[kf(t), row], lsem.at[1 + t]).wait()


OUTER_ROWS = (128, 384, 512, 512, 512)


def outer_kernel(dr_ref, dc_ref, occ_ref, vir_ref, evir_ref, eocc_ref, out_hbm, ch, cl, ecol, erow, obuf, sem):
    for k in range(2):
        for r in range(8):
            h, l = split(dc_ref[k, r])
            ch[k * 128:(k + 1) * 128, r * 128:(r + 1) * 128] = h
            cl[k * 128:(k + 1) * 128, r * 128:(r + 1) * 128] = l
    row, col = lax.axis_index("row"), lax.axis_index("col")
    occ_rows, vir_rows = [], []
    for first, size in ((row * 16, 16), (col * 8, 8)):
        at = pl.ds(pl.multiple_of(first, 8), size)
        occ_rows.append(occ_ref[at])
        vir_rows.append(vir_ref[at])
    occ = jnp.concatenate(occ_rows, axis=0)
    vir = jnp.concatenate(vir_rows, axis=0)
    low, high = vir & 127, vir >> 7
    picked = jnp.zeros((24, 128), F32)
    for h in range(16):
        table = jnp.broadcast_to(evir_ref[h:h + 1], (24, 128))
        got = jnp.take_along_axis(table, low, axis=1, mode="promise_in_bounds")
        picked = jnp.where(high == h, got, picked)
    taken = jnp.zeros((24, 128), F32)
    for o in range(64):
        taken = jnp.where(occ == o, eocc_ref[o], taken)
    negative = taken - picked
    erow[...] = negative[16:24]
    for i in range(16):
        ecol[i * 128:(i + 1) * 128] = jnp.broadcast_to(negative[i:i + 1], (128, 128)).T

    copies = []
    first = 0
    for i, size in enumerate(OUTER_ROWS):
        rows = slice(first, first + size)
        x = jnp.concatenate([dr_ref[0, rows], dr_ref[1, rows]], axis=1)
        h, l = split(x)
        acc = jnp.dot(h, ch[...], preferred_element_type=F32)
        acc += jnp.dot(l, ch[...], preferred_element_type=F32)
        acc += jnp.dot(h, cl[...], preferred_element_type=F32)
        e = ecol[rows]
        for n in range(8):
            lanes = slice(n * 128, (n + 1) * 128)
            obuf[rows, lanes] = acc[:, lanes] / (e + erow[n:n + 1])
        copies.append(pltpu.make_async_copy(obuf.at[rows], out_hbm.at[rows], sem.at[i]))
        copies[-1].start()
        first += size
    for c in copies:
        c.wait()


def local(amplitudes, factors, occ_index, vir_index, occ_energy, vir_energy):
    hbm = pl.BlockSpec(memory_space=pl.ANY)
    vmem = lambda *shape: pltpu.VMEM(shape, F32)
    dr, dc = pl.pallas_call(
        exchange_kernel,
        out_shape=(
            jax.ShapeDtypeStruct((2, 2, 8, 128, 128), F32),
            jax.ShapeDtypeStruct((2, 8, 128, 128), F32),
        ),
        in_specs=[hbm, pl.BlockSpec(memory_space=pltpu.HBM)],
        out_specs=(hbm, hbm),
        scratch_shapes=[
            vmem(2048, 1024),
            pltpu.VMEM((4, 2048, 256), BF16),
            pltpu.VMEM((4, 2048, 256), BF16),
            vmem(2, 4, 2, 16, 2048),
            pltpu.VMEM((256, 2048), BF16),
            vmem(2, 4, 2, 128, 128),
            vmem(2, 2, 64, 128),
            vmem(2, 2, 64, 128),
            vmem(2, 2, 128, 128),
            vmem(2, 2, 128, 128),
            vmem(2, 128, 128),
            vmem(2, 128, 128),
            vmem(2, 128, 128),
            vmem(2, 128, 128),
            pltpu.SemaphoreType.DMA((len(NAMES),)),
            pltpu.SemaphoreType.DMA((len(NAMES),)),
            pltpu.SemaphoreType.DMA((8,)),
            pltpu.SemaphoreType.DMA((3,)),
            pltpu.SemaphoreType.DMA((2,)),
        ],
        compiler_params=pltpu.CompilerParams(
            collective_id=0, has_side_effects=True, vmem_limit_bytes=48 * 1024 * 1024),
        name="exchange",
    )(amplitudes, factors.T)
    in_vmem = pl.BlockSpec(memory_space=pltpu.VMEM)
    return pl.pallas_call(
        outer_kernel,
        out_shape=jax.ShapeDtypeStruct((2048, 1024), F32),
        in_specs=[in_vmem] * 5 + [pl.BlockSpec(memory_space=pltpu.SMEM)],
        out_specs=hbm,
        scratch_shapes=[
            pltpu.VMEM((256, 1024), BF16),
            pltpu.VMEM((256, 1024), BF16),
            vmem(2048, 128),
            vmem(8, 128),
            vmem(2048, 1024),
            pltpu.SemaphoreType.DMA((len(OUTER_ROWS),)),
        ],
        compiler_params=pltpu.CompilerParams(vmem_limit_bytes=32 * 1024 * 1024),
        name="outer",
    )(
        dr.reshape(2, 2048, 128), dc, occ_index.reshape(128, 128), vir_index.reshape(128, 128),
        vir_energy.reshape(16, 128), occ_energy,
    )


def solution(mesh):
    return jax.shard_map(
        local,
        mesh=mesh,
        in_specs=(P("row", "col"), P("row", "col"), P(), P(), P(), P()),
        out_specs=P("row", "col"),
        check_vma=False,
    )
```

```python
import functools

import jax
import jax.numpy as jnp
from jax import lax
from jax.experimental import pallas as pl
from jax.experimental.pallas import tpu as pltpu
from jax.sharding import PartitionSpec as P

MESH = pl.DeviceIdType.MESH
F32 = jnp.float32
BF16 = jnp.bfloat16
RING = ("pA", "mB", "pB", "mA", "fA", "fB")
NAMES = ["fx"]
for t_ in range(2):
    for r_ in ("f0", "f1"):
        NAMES += [f"{r_}{m_}" for m_ in RING if t_ == 0]
    for r_ in ("c0", "c1", "r0", "r1"):
        NAMES += [f"{r_}{t_}{m_}" for m_ in RING]
    NAMES += [f"{q_}{t_}{j_}" for q_ in ("sf", "sr", "sq") for j_ in ("0", "m", "p", "2")]
    NAMES += [f"{m_}{t_}" for m_ in ("s1p", "s1m", "s2pA", "s2pB", "s2mA", "s2mB", "s3", "cx", "sw", "sx")]
ID = {n_: i_ for i_, n_ in enumerate(NAMES)}

ORDER = (
    "f0.own", "spA0", "spA1", "spA2", "spA3", "f0.fA", "f0.fB", "f0.nm", "f0.np", "f1.own", "f0.far", "spF0",
    "mm0.2", "mm0.p", "f1.fA", "f1.fB", "mm0.m", "mm0.0", "f1.nm", "f1.np", "rl0p", "rl0m", "f1.far", "spF1",
    "mm1.2", "mm1.p", "mm1.m", "mm1.0", "cr0", "rl1p", "rl1m", "c00.own", "cr1", "c10.own", "c00.fA", "c00.fB",
    "c01.own", "r00.own", "c00.nm", "c00.np", "c10.fA", "c10.fB", "r10.own", "c10.nm", "c10.np", "c00.far",
    "c11.own", "r00.fA", "r00.fB", "c01.fA", "c01.fB", "r00.nm", "r00.np", "c01.nm", "c01.np", "r01.own",
    "r10.fA", "r10.fB", "c10.far", "r10.nm", "r10.np", "r11.own", "c11.fA", "c11.fB", "r00.far", "c11.nm",
    "c11.np", "r01.fA", "r01.fB", "c01.far", "r01.nm", "r01.np", "c11.far", "r10.far", "r11.fA", "r11.fB",
    "rf0", "r11.nm", "r11.np", "r01.far", "r11.far", "rf1",
)


def split(v):
    hi = v.astype(BF16)
    return hi, (v - hi.astype(F32)).astype(BF16)


def exchange_kernel(
    a_hbm, f_hbm, dr, dc,
    abuf, ah, al, ft, fhl, pt, r1a, r1b, r2p, r2m, sx, r3, dp, dn,
    ssem, rsem, asem, lsem, msem,
):
    row, col = lax.axis_index("row"), lax.axis_index("col")
    x_lo, z = row // 4, row % 4
    s = col // 2
    x_hi, y, core = s // 4, s % 4, col % 2

    def dev(xh, xl, yy, zz, cc):
        return (xl * 4 + zz, xh * 8 + yy * 2 + cc)

    yp, ym, y2 = (y + 1) % 4, (y + 3) % 4, (y + 2) % 4
    zp, zm, z2 = (z + 1) % 4, (z + 3) % 4, (z + 2) % 4
    d_yp, d_ym = dev(x_hi, x_lo, yp, z, core), dev(x_hi, x_lo, ym, z, core)
    d_zp, d_zm = dev(x_hi, x_lo, y, zp, core), dev(x_hi, x_lo, y, zm, core)
    d_x2 = dev(1 - x_hi, x_lo, y, z, core)
    d_xn = dev(x_hi, 1 - x_lo, y, z, core)
    d_sib = dev(x_hi, x_lo, y, z, 1 - core)
    d_tr = dev(x_lo, x_hi, (y + z) % 4, y, core)
    d_from_tr = dev(x_lo, x_hi, z, (y - z + 4) % 4, core)
    d_tx = dev(1 - x_lo, x_hi, (y + z) % 4, y, core)
    d_from_tx = dev(x_lo, 1 - x_hi, z, (y - z + 4) % 4, core)
    stays = (x_hi == x_lo) & (y == 0) & (z == 0)
    moves = jnp.logical_not(stays)
    diag = row == s

    sends, got = {}, set()

    def make(name, src, dst, to):
        i = ID[name]
        return pltpu.make_async_remote_copy(
            src_ref=src, dst_ref=dst, send_sem=ssem.at[i], recv_sem=rsem.at[i],
            device_id=to, device_id_type=MESH)

    def start(name, src, dst, to):
        sends[name] = make(name, src, dst, to)
        sends[name].start()

    def recv(name, ref):
        if name not in got:
            got.add(name)
            make(name, ref, ref, d_sib).wait_recv()

    steps = {}

    def step(name):
        def keep(f):
            steps[name] = f
        return keep

    def ring(n, slot, pos, to_up, to_down, half, own, sib=None):
        u, d, o = (pos + 1) % 4, (pos + 3) % 4, (pos + 2) % 4

        def part(i, which):
            return slot(i).at[pl.ds(which * half, half)]

        def to_sib(tag, i):
            if sib is not None:
                start(sib + tag, slot(i), slot(i), d_sib)

        def send_own(src=None):
            src = slot(pos) if src is None else src
            for m, w, to in (("pA", 0, to_up), ("mB", 1, to_down), ("pB", 1, to_up), ("mA", 0, to_down)):
                start(n + m, src.at[pl.ds(w * half, half)], part(pos, w), to)
            if sib is not None:
                start(sib + "0", src, slot(pos), d_sib)

        @step(n + ".own")
        def _():
            own(send_own)

        @step(n + ".fA")
        def _():
            recv(n + "pA", part(d, 0))
            start(n + "fA", part(d, 0), part(d, 0), to_up)

        @step(n + ".fB")
        def _():
            recv(n + "mB", part(u, 1))
            start(n + "fB", part(u, 1), part(u, 1), to_down)

        @step(n + ".nm")
        def _():
            recv(n + "pA", part(d, 0))
            recv(n + "pB", part(d, 1))
            to_sib("m", d)

        @step(n + ".np")
        def _():
            recv(n + "mA", part(u, 0))
            recv(n + "mB", part(u, 1))
            to_sib("p", u)

        @step(n + ".far")
        def _():
            recv(n + "fA", part(o, 0))
            recv(n + "fB", part(o, 1))
            to_sib("2", o)

    def a_copy(i):
        rows = pl.ds(i * 256, 256)
        return pltpu.make_async_copy(a_hbm.at[rows], abuf.at[rows], asem.at[i])

    for i in range(8):
        a_copy(i).start()
    own_f = pltpu.make_async_copy(f_hbm, ft.at[x_hi, y, core], lsem.at[0])
    own_f.start()

    barrier = pltpu.get_barrier_semaphore()
    for d in (d_yp, d_ym, d_zp, d_zm, d_x2, d_xn, d_sib, d_from_tx):
        pl.semaphore_signal(barrier, inc=1, device_id=d, device_id_type=MESH)

    @pl.when(moves)
    def _():
        pl.semaphore_signal(barrier, inc=1, device_id=d_from_tr, device_id_type=MESH)
        pl.semaphore_wait(barrier, 9)

    @pl.when(stays)
    def _():
        pl.semaphore_wait(barrier, 8)

    def kf(t):
        return x_hi if t == 0 else 1 - x_hi

    def kr(t):
        return x_lo if t == 0 else 1 - x_lo

    def own_f0(send):
        start("fx", f_hbm, ft.at[x_hi, y, core], d_x2)
        send(f_hbm)

    def own_f1(send):
        recv("fx", ft.at[1 - x_hi, y, core])
        send()

    for t, own in enumerate((own_f0, own_f1)):
        ring(f"f{t}", lambda i, t=t: ft.at[kf(t), i, core], y, d_yp, d_ym, 8, own, f"sf{t}")

    for q in range(4):
        @step(f"spA{q}")
        def _(q=q):
            def body(i, carry):
                a_copy(i).wait()
                rows = pl.ds(pl.multiple_of(i * 256, 256), 256)
                for xl in range(2):
                    for zz in range(4):
                        r = xl * 4 + zz
                        h, l = split(abuf[rows, r * 128:(r + 1) * 128])
                        ah[zz, rows, xl * 128:(xl + 1) * 128] = h
                        al[zz, rows, xl * 128:(xl + 1) * 128] = l
                return carry
            lax.fori_loop(2 * q, 2 * q + 2, body, 0)

    up, down = pl.ds(0, 64), pl.ds(64, 64)

    def product(t, zz):
        h = kf(t)
        both = jnp.dot(fhl[...], ah[zz], preferred_element_type=F32)
        low = jnp.dot(fhl[0:128], al[zz], preferred_element_type=F32)
        p = both[:128] + (both[128:] + low)
        for xl in range(2):
            pt[t, zz, xl] = p[:, xl * 128:(xl + 1) * 128]

        @pl.when(diag)
        def _():
            for xl in range(2):
                at = pl.multiple_of(core * 1024 + (xl * 4 + zz) * 128, 128)
                pt[t, zz, xl] += ft[h, :, :, :, pl.ds(at, 128)].reshape(128, 128)

    for t in range(2):
        @step(f"spF{t}")
        def _(t=t):
            if t == 0:
                own_f.wait()
            for j, pos in (("0", y), ("m", ym), ("p", yp), ("2", y2)):
                recv(f"sf{t}{j}", ft.at[kf(t), pos, 1 - core])
            hi, lo = split(ft[kf(t)].reshape(128, 2048))
            fhl[0:128] = hi
            fhl[128:256] = lo

        @step(f"mm{t}.2")
        def _(t=t):
            product(t, z2)
            start(f"s1p{t}", pt.at[t, z2, :, up], r1a.at[t], d_zp)
            start(f"s1m{t}", pt.at[t, z2, :, down], r1b.at[t], d_zm)

        @step(f"mm{t}.p")
        def _(t=t):
            product(t, zp)
            start(f"s2pB{t}", pt.at[t, zp, :, down], r2p.at[t, :, down], d_zp)

        @step(f"mm{t}.m")
        def _(t=t):
            product(t, zm)
            start(f"s2mA{t}", pt.at[t, zm, :, up], r2m.at[t, :, up], d_zm)

        @step(f"mm{t}.0")
        def _(t=t):
            product(t, z)

        @step(f"rl{t}p")
        def _(t=t):
            recv(f"s1p{t}", r1a.at[t])
            pt[t, zp, :, 0:64] += r1a[t]
            start(f"s2pA{t}", pt.at[t, zp, :, up], r2p.at[t, :, up], d_zp)

        @step(f"rl{t}m")
        def _(t=t):
            recv(f"s1m{t}", r1b.at[t])
            pt[t, zm, :, 64:128] += r1b[t]
            start(f"s2mB{t}", pt.at[t, zm, :, down], r2m.at[t, :, down], d_zm)

        @step(f"cr{t}")
        def _(t=t):
            recv(f"s2pA{t}", r2p.at[t, :, up])
            recv(f"s2pB{t}", r2p.at[t, :, down])
            recv(f"s2mA{t}", r2m.at[t, :, up])
            recv(f"s2mB{t}", r2m.at[t, :, down])
            o = 1 - x_lo
            sx[t] = pt[t, z, o] + r2p[t, o] + r2m[t, o]
            start(f"s3{t}", sx.at[t], r3.at[t], d_xn)

        def own_c0(send, t=t):
            own = pt[t, z, x_lo] + r2p[t, x_lo] + r2m[t, x_lo]
            recv(f"s3{t}", r3.at[t])
            d = own + r3[t]
            dn[t] = d.T
            start(f"sx{t}", dn.at[t], dr.at[kf(t), core, row], d_tx)

            @pl.when(moves)
            def _():
                make(f"sw{t}", dn.at[t], dr.at[kf(t), core, row], d_tr).start()

            @pl.when(stays)
            def _():
                pltpu.make_async_copy(dn.at[t], dr.at[kf(t), core, row], msem.at[t]).start()

            dp[t] = d
            start(f"cx{t}", dp.at[t], dc.at[kf(t), row], d_xn)
            send(dp.at[t])
            pltpu.make_async_copy(dp.at[t], dc.at[kf(t), row], lsem.at[1 + t]).start()

        def own_c1(send, t=t):
            recv(f"cx{t}", dc.at[kf(t), (1 - x_lo) * 4 + z])
            send()

        def own_r0(send, t=t):
            mine = dr.at[kr(t), core, x_hi * 4 + (y - z + 4) % 4]

            @pl.when(moves)
            def _():
                make(f"sw{t}", mine, mine, d_sib).wait_recv()

            @pl.when(stays)
            def _():
                pltpu.make_async_copy(dn.at[t], mine, msem.at[t]).wait()

            send()

        def own_r1(send, t=t):
            recv(f"sx{t}", dr.at[kr(t), core, (1 - x_hi) * 4 + (y - z + 4) % 4])
            send()

        for j, own in enumerate((own_c0, own_c1)):
            xl = x_lo if j == 0 else 1 - x_lo
            ring(f"c{j}{t}", lambda i, t=t, xl=xl: dc.at[kf(t), xl * 4 + i], z, d_zp, d_zm, 64, own)
        for j, own in enumerate((own_r0, own_r1)):
            xh = x_hi if j == 0 else 1 - x_hi
            ring(f"r{j}{t}", lambda i, t=t, xh=xh: dr.at[kr(t), core, xh * 4 + (i - z + 4) % 4], y, d_yp, d_ym, 64, own,
                 f"{'sr' if j == 0 else 'sq'}{t}")

        @step(f"rf{t}")
        def _(t=t):
            for j in range(2):
                xh = x_hi if j == 0 else 1 - x_hi
                for tag, pos in (("0", y), ("m", ym), ("p", yp), ("2", y2)):
                    recv(f"{'sr' if j == 0 else 'sq'}{t}{tag}", dr.at[kr(t), 1 - core, xh * 4 + (pos - z + 4) % 4])

    for name in ORDER:
        steps[name]()

    for c in sends.values():
        c.wait_send()

    @pl.when(moves)
    def _():
        for t in range(2):
            make(f"sw{t}", dn.at[t], dr.at[kf(t), core, row], d_tr).wait_send()

    for t in range(2):
        pltpu.make_async_copy(dp.at[t], dc.at[kf(t), row], lsem.at[1 + t]).wait()


OUTER_ROWS = (128, 384, 512, 512, 512)


def outer_kernel(dr_ref, dc_ref, occ_ref, vir_ref, evir_ref, eocc_ref, out_hbm, ch, cl, ecol, erow, obuf, sem):
    for k in range(2):
        for r in range(8):
            h, l = split(dc_ref[k, r])
            ch[k * 128:(k + 1) * 128, r * 128:(r + 1) * 128] = h
            cl[k * 128:(k + 1) * 128, r * 128:(r + 1) * 128] = l
    row, col = lax.axis_index("row"), lax.axis_index("col")
    occ_rows, vir_rows = [], []
    for first, size in ((row * 16, 16), (col * 8, 8)):
        at = pl.ds(pl.multiple_of(first, 8), size)
        occ_rows.append(occ_ref[at])
        vir_rows.append(vir_ref[at])
    occ = jnp.concatenate(occ_rows, axis=0)
    vir = jnp.concatenate(vir_rows, axis=0)
    low, high = vir & 127, vir >> 7
    picked = jnp.zeros((24, 128), F32)
    for h in range(16):
        table = jnp.broadcast_to(evir_ref[h:h + 1], (24, 128))
        got = jnp.take_along_axis(table, low, axis=1, mode="promise_in_bounds")
        picked = jnp.where(high == h, got, picked)
    taken = jnp.zeros((24, 128), F32)
    for o in range(64):
        taken = jnp.where(occ == o, eocc_ref[o], taken)
    negative = taken - picked
    erow[...] = negative[16:24]
    for i in range(16):
        ecol[i * 128:(i + 1) * 128] = jnp.broadcast_to(negative[i:i + 1], (128, 128)).T

    copies = []
    first = 0
    for i, size in enumerate(OUTER_ROWS):
        rows = slice(first, first + size)
        x = jnp.concatenate([dr_ref[0, rows], dr_ref[1, rows]], axis=1)
        h, l = split(x)
        acc = jnp.dot(h, ch[...], preferred_element_type=F32)
        acc += jnp.dot(l, ch[...], preferred_element_type=F32)
        acc += jnp.dot(h, cl[...], preferred_element_type=F32)
        e = ecol[rows]
        for n in range(8):
            lanes = slice(n * 128, (n + 1) * 128)
            obuf[rows, lanes] = acc[:, lanes] / (e + erow[n:n + 1])
        copies.append(pltpu.make_async_copy(obuf.at[rows], out_hbm.at[rows], sem.at[i]))
        copies[-1].start()
        first += size
    for c in copies:
        c.wait()


def local(amplitudes, factors, occ_index, vir_index, occ_energy, vir_energy):
    hbm = pl.BlockSpec(memory_space=pl.ANY)
    vmem = lambda *shape: pltpu.VMEM(shape, F32)
    dr, dc = pl.pallas_call(
        exchange_kernel,
        out_shape=(
            jax.ShapeDtypeStruct((2, 2, 8, 128, 128), F32),
            jax.ShapeDtypeStruct((2, 8, 128, 128), F32),
        ),
        in_specs=[hbm, pl.BlockSpec(memory_space=pltpu.HBM)],
        out_specs=(hbm, hbm),
        scratch_shapes=[
            vmem(2048, 1024),
            pltpu.VMEM((4, 2048, 256), BF16),
            pltpu.VMEM((4, 2048, 256), BF16),
            vmem(2, 4, 2, 16, 2048),
            pltpu.VMEM((256, 2048), BF16),
            vmem(2, 4, 2, 128, 128),
            vmem(2, 2, 64, 128),
            vmem(2, 2, 64, 128),
            vmem(2, 2, 128, 128),
            vmem(2, 2, 128, 128),
            vmem(2, 128, 128),
            vmem(2, 128, 128),
            vmem(2, 128, 128),
            vmem(2, 128, 128),
            pltpu.SemaphoreType.DMA((len(NAMES),)),
            pltpu.SemaphoreType.DMA((len(NAMES),)),
            pltpu.SemaphoreType.DMA((8,)),
            pltpu.SemaphoreType.DMA((3,)),
            pltpu.SemaphoreType.DMA((2,)),
        ],
        compiler_params=pltpu.CompilerParams(
            collective_id=0, has_side_effects=True, vmem_limit_bytes=48 * 1024 * 1024),
        name="exchange",
    )(amplitudes, factors.T)
    in_vmem = pl.BlockSpec(memory_space=pltpu.VMEM)
    return pl.pallas_call(
        outer_kernel,
        out_shape=jax.ShapeDtypeStruct((2048, 1024), F32),
        in_specs=[in_vmem] * 5 + [pl.BlockSpec(memory_space=pltpu.SMEM)],
        out_specs=hbm,
        scratch_shapes=[
            pltpu.VMEM((256, 1024), BF16),
            pltpu.VMEM((256, 1024), BF16),
            vmem(2048, 128),
            vmem(8, 128),
            vmem(2048, 1024),
            pltpu.SemaphoreType.DMA((len(OUTER_ROWS),)),
        ],
        compiler_params=pltpu.CompilerParams(vmem_limit_bytes=32 * 1024 * 1024),
        name="outer",
    )(
        dr.reshape(2, 2048, 128), dc, occ_index.reshape(128, 128), vir_index.reshape(128, 128),
        vir_energy.reshape(16, 128), occ_energy,
    )


def solution(mesh):
    return jax.shard_map(
        local,
        mesh=mesh,
        in_specs=(P("row", "col"), P("row", "col"), P(), P(), P(), P()),
        out_specs=P("row", "col"),
        check_vma=False,
    )
```

```python
import functools

import jax
import jax.numpy as jnp
from jax import lax
from jax.experimental import pallas as pl
from jax.experimental.pallas import tpu as pltpu
from jax.sharding import PartitionSpec as P

MESH = pl.DeviceIdType.MESH
F32 = jnp.float32
BF16 = jnp.bfloat16
RING = ("pA", "mB", "pB", "mA", "fA", "fB")
NAMES = ["fx", "fy"]
for t_ in range(2):
    for r_ in ("f0", "f1"):
        NAMES += [f"{r_}{m_}" for m_ in RING if t_ == 0 and (r_ == "f0" or m_[0] != "f")]
    for r_ in ("c0", "c1", "r0", "r1"):
        NAMES += [f"{r_}{t_}{m_}" for m_ in RING]
    NAMES += [f"{q_}{t_}{j_}" for q_ in ("sf", "sr", "sq") for j_ in ("0", "m", "p", "2")]
    NAMES += [f"{m_}{t_}" for m_ in ("s1p", "s1m", "s2pA", "s2pB", "s2mA", "s2mB", "s3", "cx", "sw", "sx")]
ID = {n_: i_ for i_, n_ in enumerate(NAMES)}

ORDER = (
    "f0.own", "spA", "f0.fA", "f0.fB", "f0.nm", "f0.np", "f1.own", "f0.far", "spF0", "mm0", "f1.nm", "f1.np",
    "f1.far", "rl0p", "rl0m", "spF1", "mm1", "cr0", "rl1p", "rl1m", "c00.own", "cr1", "c10.own", "c00.fA",
    "c00.fB", "c00.nm", "c01.own", "c00.np", "r00.own", "c10.fA", "c10.fB", "c10.nm", "c10.np", "c00.far",
    "c11.own", "r00.fA", "r00.fB", "c01.fA", "c01.fB", "r01.own", "r10.own", "r00.nm", "r00.np", "c01.nm",
    "c01.np", "c10.far", "r11.own", "r00.far", "c11.fA", "c11.fB", "r01.fA", "r01.fB", "c11.nm", "c11.np",
    "r01.nm", "r01.np", "c01.far", "r10.fA", "r10.fB", "c11.far", "r10.nm", "r10.np", "r11.fA", "r11.fB",
    "r11.nm", "r11.np", "r01.far", "r10.far", "r11.far", "rf0", "rf1",
)


def split(v):
    hi = v.astype(BF16)
    return hi, (v - hi.astype(F32)).astype(BF16)


def exchange_kernel(
    a_hbm, f_hbm, dr, dc,
    abuf, ah, al, ft, fhl, pt, r1a, r1b, r2p, r2m, sx, r3, dp, dn,
    ssem, rsem, asem, lsem, msem,
):
    row, col = lax.axis_index("row"), lax.axis_index("col")
    x_lo, z = row // 4, row % 4
    s = col // 2
    x_hi, y, core = s // 4, s % 4, col % 2

    def dev(xh, xl, yy, zz, cc):
        return (xl * 4 + zz, xh * 8 + yy * 2 + cc)

    yp, ym, y2 = (y + 1) % 4, (y + 3) % 4, (y + 2) % 4
    zp, zm, z2 = (z + 1) % 4, (z + 3) % 4, (z + 2) % 4
    d_yp, d_ym = dev(x_hi, x_lo, yp, z, core), dev(x_hi, x_lo, ym, z, core)
    d_zp, d_zm = dev(x_hi, x_lo, y, zp, core), dev(x_hi, x_lo, y, zm, core)
    d_x2 = dev(1 - x_hi, x_lo, y, z, core)
    d_xn = dev(x_hi, 1 - x_lo, y, z, core)
    d_sib = dev(x_hi, x_lo, y, z, 1 - core)
    d_tr = dev(x_lo, x_hi, (y + z) % 4, y, core)
    d_from_tr = dev(x_lo, x_hi, z, (y - z + 4) % 4, core)
    d_tx = dev(1 - x_lo, x_hi, (y + z) % 4, y, core)
    d_from_tx = dev(x_lo, 1 - x_hi, z, (y - z + 4) % 4, core)
    stays = (x_hi == x_lo) & (y == 0) & (z == 0)
    moves = jnp.logical_not(stays)
    diag = row == s

    sends, got = {}, set()

    def make(name, src, dst, to):
        i = ID[name]
        return pltpu.make_async_remote_copy(
            src_ref=src, dst_ref=dst, send_sem=ssem.at[i], recv_sem=rsem.at[i],
            device_id=to, device_id_type=MESH)

    def start(name, src, dst, to):
        sends[name] = make(name, src, dst, to)
        sends[name].start()

    def recv(name, ref):
        if name not in got:
            got.add(name)
            make(name, ref, ref, d_sib).wait_recv()

    steps = {}

    def step(name):
        def keep(f):
            steps[name] = f
        return keep

    def ring(n, slot, pos, to_up, to_down, half, own, sib=None, far=None):
        u, d, o = (pos + 1) % 4, (pos + 3) % 4, (pos + 2) % 4

        def part(i, which):
            return slot(i).at[pl.ds(which * half, half)]

        def to_sib(tag, i):
            if sib is not None:
                start(sib + tag, slot(i), slot(i), d_sib)

        def send_own(src=None):
            src = slot(pos) if src is None else src
            for m, w, to in (("pA", 0, to_up), ("mB", 1, to_down), ("pB", 1, to_up), ("mA", 0, to_down)):
                start(n + m, src.at[pl.ds(w * half, half)], part(pos, w), to)
            if sib is not None:
                start(sib + "0", src, slot(pos), d_sib)

        @step(n + ".own")
        def _():
            own(send_own)

        if far is None:
            @step(n + ".fA")
            def _():
                recv(n + "pA", part(d, 0))
                start(n + "fA", part(d, 0), part(d, 0), to_up)

            @step(n + ".fB")
            def _():
                recv(n + "mB", part(u, 1))
                start(n + "fB", part(u, 1), part(u, 1), to_down)

        @step(n + ".nm")
        def _():
            recv(n + "pA", part(d, 0))
            recv(n + "pB", part(d, 1))
            to_sib("m", d)

        @step(n + ".np")
        def _():
            recv(n + "mA", part(u, 0))
            recv(n + "mB", part(u, 1))
            to_sib("p", u)

        @step(n + ".far")
        def _():
            if far is None:
                recv(n + "fA", part(o, 0))
                recv(n + "fB", part(o, 1))
            else:
                recv(far, slot(o))
            if n == "f0":
                start("fy", slot(o), slot(o), d_x2)
            to_sib("2", o)

    def a_copy(i):
        rows = pl.ds(i * 256, 256)
        return pltpu.make_async_copy(a_hbm.at[rows], abuf.at[rows], asem.at[i])

    for i in range(8):
        a_copy(i).start()
    own_f = pltpu.make_async_copy(f_hbm, ft.at[x_hi, y, core], lsem.at[0])
    own_f.start()

    barrier = pltpu.get_barrier_semaphore()
    for d in (d_yp, d_ym, d_zp, d_zm, d_x2, d_xn, d_sib, d_from_tx):
        pl.semaphore_signal(barrier, inc=1, device_id=d, device_id_type=MESH)

    @pl.when(moves)
    def _():
        pl.semaphore_signal(barrier, inc=1, device_id=d_from_tr, device_id_type=MESH)
        pl.semaphore_wait(barrier, 9)

    @pl.when(stays)
    def _():
        pl.semaphore_wait(barrier, 8)

    def kf(t):
        return x_hi if t == 0 else 1 - x_hi

    def kr(t):
        return x_lo if t == 0 else 1 - x_lo

    def own_f0(send):
        start("fx", f_hbm, ft.at[x_hi, y, core], d_x2)
        send(f_hbm)

    def own_f1(send):
        recv("fx", ft.at[1 - x_hi, y, core])
        send()

    for t, own in enumerate((own_f0, own_f1)):
        ring(f"f{t}", lambda i, t=t: ft.at[kf(t), i, core], y, d_yp, d_ym, 8, own, f"sf{t}",
             "fy" if t == 1 else None)

    @step("spA")
    def _():
        def body(i, carry):
            a_copy(i).wait()
            rows = pl.ds(pl.multiple_of(i * 256, 256), 256)
            for xl in range(2):
                for zz in range(4):
                    r = xl * 4 + zz
                    h, l = split(abuf[rows, r * 128:(r + 1) * 128])
                    ah[zz, rows, xl * 128:(xl + 1) * 128] = h
                    al[zz, rows, xl * 128:(xl + 1) * 128] = l
            return carry
        lax.fori_loop(0, 8, body, 0)

    up, down = pl.ds(0, 64), pl.ds(64, 64)

    def product(t, zz):
        h = kf(t)
        both = jnp.dot(fhl[...], ah[zz], preferred_element_type=F32)
        low = jnp.dot(fhl[0:128], al[zz], preferred_element_type=F32)
        p = both[:128] + (both[128:] + low)
        for xl in range(2):
            pt[t, zz, xl] = p[:, xl * 128:(xl + 1) * 128]

        @pl.when(diag)
        def _():
            for xl in range(2):
                at = pl.multiple_of(core * 1024 + (xl * 4 + zz) * 128, 128)
                pt[t, zz, xl] += ft[h, :, :, :, pl.ds(at, 128)].reshape(128, 128)

    for t in range(2):
        @step(f"spF{t}")
        def _(t=t):
            if t == 0:
                own_f.wait()
            for j, pos in (("0", y), ("m", ym), ("p", yp), ("2", y2)):
                recv(f"sf{t}{j}", ft.at[kf(t), pos, 1 - core])
            hi, lo = split(ft[kf(t)].reshape(128, 2048))
            fhl[0:128] = hi
            fhl[128:256] = lo

        @step(f"mm{t}")
        def _(t=t):
            first = [
                make(f"s1p{t}", pt.at[t, z2, :, up], r1a.at[t], d_zp),
                make(f"s1m{t}", pt.at[t, z2, :, down], r1b.at[t], d_zm),
            ]
            above = make(f"s2pB{t}", pt.at[t, zp, :, down], r2p.at[t, :, down], d_zp)
            below = make(f"s2mA{t}", pt.at[t, zm, :, up], r2m.at[t, :, up], d_zm)
            sends.update({f"s1p{t}": first[0], f"s1m{t}": first[1], f"s2pB{t}": above, f"s2mA{t}": below})

            def body(i, carry):
                zz = jnp.where(i == 0, z2, jnp.where(i == 1, zp, jnp.where(i == 2, zm, z)))
                product(t, zz)

                @pl.when(i == 0)
                def _():
                    first[0].start()
                    first[1].start()

                @pl.when(i == 1)
                def _():
                    above.start()

                @pl.when(i == 2)
                def _():
                    below.start()

                return carry

            lax.fori_loop(0, 4, body, 0)

        @step(f"rl{t}p")
        def _(t=t):
            recv(f"s1p{t}", r1a.at[t])
            pt[t, zp, :, 0:64] += r1a[t]
            start(f"s2pA{t}", pt.at[t, zp, :, up], r2p.at[t, :, up], d_zp)

        @step(f"rl{t}m")
        def _(t=t):
            recv(f"s1m{t}", r1b.at[t])
            pt[t, zm, :, 64:128] += r1b[t]
            start(f"s2mB{t}", pt.at[t, zm, :, down], r2m.at[t, :, down], d_zm)

        @step(f"cr{t}")
        def _(t=t):
            recv(f"s2pA{t}", r2p.at[t, :, up])
            recv(f"s2pB{t}", r2p.at[t, :, down])
            recv(f"s2mA{t}", r2m.at[t, :, up])
            recv(f"s2mB{t}", r2m.at[t, :, down])
            o = 1 - x_lo
            sx[t] = pt[t, z, o] + r2p[t, o] + r2m[t, o]
            start(f"s3{t}", sx.at[t], r3.at[t], d_xn)

        def own_c0(send, t=t):
            own = pt[t, z, x_lo] + r2p[t, x_lo] + r2m[t, x_lo]
            recv(f"s3{t}", r3.at[t])
            d = own + r3[t]
            dn[t] = d.T
            if t == 1:
                start(f"sx{t}", dn.at[t], dr.at[kf(t), core, row], d_tx)

            @pl.when(moves)
            def _():
                make(f"sw{t}", dn.at[t], dr.at[kf(t), core, row], d_tr).start()

            @pl.when(stays)
            def _():
                pltpu.make_async_copy(dn.at[t], dr.at[kf(t), core, row], msem.at[t]).start()

            dp[t] = d
            start(f"cx{t}", dp.at[t], dc.at[kf(t), row], d_xn)
            send(dp.at[t])
            pltpu.make_async_copy(dp.at[t], dc.at[kf(t), row], lsem.at[1 + t]).start()

        def own_c1(send, t=t):
            recv(f"cx{t}", dc.at[kf(t), (1 - x_lo) * 4 + z])
            send()

        def own_r0(send, t=t):
            mine = dr.at[kr(t), core, x_hi * 4 + (y - z + 4) % 4]

            @pl.when(moves)
            def _():
                make(f"sw{t}", mine, mine, d_sib).wait_recv()

            @pl.when(stays)
            def _():
                pltpu.make_async_copy(dn.at[t], mine, msem.at[t]).wait()

            if t == 0:
                start(f"sx{t}", mine, mine, d_x2)
            send()

        def own_r1(send, t=t):
            recv(f"sx{t}", dr.at[kr(t), core, (1 - x_hi) * 4 + (y - z + 4) % 4])
            send()

        for j, own in enumerate((own_c0, own_c1)):
            xl = x_lo if j == 0 else 1 - x_lo
            ring(f"c{j}{t}", lambda i, t=t, xl=xl: dc.at[kf(t), xl * 4 + i], z, d_zp, d_zm, 64, own)
        for j, own in enumerate((own_r0, own_r1)):
            xh = x_hi if j == 0 else 1 - x_hi
            ring(f"r{j}{t}", lambda i, t=t, xh=xh: dr.at[kr(t), core, xh * 4 + (i - z + 4) % 4], y, d_yp, d_ym, 64, own,
                 f"{'sr' if j == 0 else 'sq'}{t}")

        @step(f"rf{t}")
        def _(t=t):
            for j in range(2):
                xh = x_hi if j == 0 else 1 - x_hi
                for tag, pos in (("0", y), ("m", ym), ("p", yp), ("2", y2)):
                    recv(f"{'sr' if j == 0 else 'sq'}{t}{tag}", dr.at[kr(t), 1 - core, xh * 4 + (pos - z + 4) % 4])

    for name in ORDER:
        steps[name]()

    for c in sends.values():
        c.wait_send()

    @pl.when(moves)
    def _():
        for t in range(2):
            make(f"sw{t}", dn.at[t], dr.at[kf(t), core, row], d_tr).wait_send()

    for t in range(2):
        pltpu.make_async_copy(dp.at[t], dc.at[kf(t), row], lsem.at[1 + t]).wait()


OUTER_ROWS = (128, 384, 512, 512, 512)


def outer_kernel(dr_ref, dc_ref, occ_ref, vir_ref, evir_ref, eocc_ref, out_hbm, ch, cl, ecol, erow, obuf, sem):
    for k in range(2):
        for r in range(8):
            h, l = split(dc_ref[k, r])
            ch[k * 128:(k + 1) * 128, r * 128:(r + 1) * 128] = h
            cl[k * 128:(k + 1) * 128, r * 128:(r + 1) * 128] = l
    row, col = lax.axis_index("row"), lax.axis_index("col")
    occ_rows, vir_rows = [], []
    for first, size in ((row * 16, 16), (col * 8, 8)):
        at = pl.ds(pl.multiple_of(first, 8), size)
        occ_rows.append(occ_ref[at])
        vir_rows.append(vir_ref[at])
    occ = jnp.concatenate(occ_rows, axis=0)
    vir = jnp.concatenate(vir_rows, axis=0)
    low, high = vir & 127, vir >> 7
    picked = jnp.zeros((24, 128), F32)
    for h in range(16):
        table = jnp.broadcast_to(evir_ref[h:h + 1], (24, 128))
        got = jnp.take_along_axis(table, low, axis=1, mode="promise_in_bounds")
        picked = jnp.where(high == h, got, picked)
    taken = jnp.zeros((24, 128), F32)
    for o in range(64):
        taken = jnp.where(occ == o, eocc_ref[o], taken)
    negative = taken - picked
    erow[...] = negative[16:24]
    for i in range(16):
        ecol[i * 128:(i + 1) * 128] = jnp.broadcast_to(negative[i:i + 1], (128, 128)).T

    copies = []
    first = 0
    for i, size in enumerate(OUTER_ROWS):
        rows = slice(first, first + size)
        x = jnp.concatenate([dr_ref[0, rows], dr_ref[1, rows]], axis=1)
        h, l = split(x)
        acc = jnp.dot(h, ch[...], preferred_element_type=F32)
        acc += jnp.dot(l, ch[...], preferred_element_type=F32)
        acc += jnp.dot(h, cl[...], preferred_element_type=F32)
        e = ecol[rows]
        for n in range(8):
            lanes = slice(n * 128, (n + 1) * 128)
            obuf[rows, lanes] = acc[:, lanes] / (e + erow[n:n + 1])
        copies.append(pltpu.make_async_copy(obuf.at[rows], out_hbm.at[rows], sem.at[i]))
        copies[-1].start()
        first += size
    for c in copies:
        c.wait()


def local(amplitudes, factors, occ_index, vir_index, occ_energy, vir_energy):
    hbm = pl.BlockSpec(memory_space=pl.ANY)
    vmem = lambda *shape: pltpu.VMEM(shape, F32)
    dr, dc = pl.pallas_call(
        exchange_kernel,
        out_shape=(
            jax.ShapeDtypeStruct((2, 2, 8, 128, 128), F32),
            jax.ShapeDtypeStruct((2, 8, 128, 128), F32),
        ),
        in_specs=[hbm, pl.BlockSpec(memory_space=pltpu.HBM)],
        out_specs=(hbm, hbm),
        scratch_shapes=[
            vmem(2048, 1024),
            pltpu.VMEM((4, 2048, 256), BF16),
            pltpu.VMEM((4, 2048, 256), BF16),
            vmem(2, 4, 2, 16, 2048),
            pltpu.VMEM((256, 2048), BF16),
            vmem(2, 4, 2, 128, 128),
            vmem(2, 2, 64, 128),
            vmem(2, 2, 64, 128),
            vmem(2, 2, 128, 128),
            vmem(2, 2, 128, 128),
            vmem(2, 128, 128),
            vmem(2, 128, 128),
            vmem(2, 128, 128),
            vmem(2, 128, 128),
            pltpu.SemaphoreType.DMA((len(NAMES),)),
            pltpu.SemaphoreType.DMA((len(NAMES),)),
            pltpu.SemaphoreType.DMA((8,)),
            pltpu.SemaphoreType.DMA((3,)),
            pltpu.SemaphoreType.DMA((2,)),
        ],
        compiler_params=pltpu.CompilerParams(
            collective_id=0, has_side_effects=True, vmem_limit_bytes=48 * 1024 * 1024),
        name="exchange",
    )(amplitudes, factors.T)
    in_vmem = pl.BlockSpec(memory_space=pltpu.VMEM)
    return pl.pallas_call(
        outer_kernel,
        out_shape=jax.ShapeDtypeStruct((2048, 1024), F32),
        in_specs=[in_vmem] * 5 + [pl.BlockSpec(memory_space=pltpu.SMEM)],
        out_specs=hbm,
        scratch_shapes=[
            pltpu.VMEM((256, 1024), BF16),
            pltpu.VMEM((256, 1024), BF16),
            vmem(2048, 128),
            vmem(8, 128),
            vmem(2048, 1024),
            pltpu.SemaphoreType.DMA((len(OUTER_ROWS),)),
        ],
        compiler_params=pltpu.CompilerParams(vmem_limit_bytes=32 * 1024 * 1024),
        name="outer",
    )(
        dr.reshape(2, 2048, 128), dc, occ_index.reshape(128, 128), vir_index.reshape(128, 128),
        vir_energy.reshape(16, 128), occ_energy,
    )


def solution(mesh):
    return jax.shard_map(
        local,
        mesh=mesh,
        in_specs=(P("row", "col"), P("row", "col"), P(), P(), P(), P()),
        out_specs=P("row", "col"),
        check_vma=False,
    )
```

```python
import functools

import jax
import jax.numpy as jnp
from jax import lax
from jax.experimental import pallas as pl
from jax.experimental.pallas import tpu as pltpu
from jax.sharding import PartitionSpec as P

MESH = pl.DeviceIdType.MESH
F32 = jnp.float32
BF16 = jnp.bfloat16
RING = ("pA", "mB", "pB", "mA", "fA", "fB")
NAMES = ["fx", "fy"]
for t_ in range(2):
    for r_ in ("f0", "f1"):
        NAMES += [f"{r_}{m_}" for m_ in RING if t_ == 0 and (r_ == "f0" or m_[0] != "f")]
    for r_ in ("c0", "c1", "r0", "r1"):
        NAMES += [f"{r_}{t_}{m_}" for m_ in RING]
    NAMES += [f"{q_}{t_}{j_}" for q_ in ("sf", "sr", "sq") for j_ in ("0", "m", "p", "2")]
    NAMES += [f"{m_}{t_}" for m_ in ("p0", "p1", "p2", "p3", "p4", "p5", "p6", "cx", "sw", "sx")]
ID = {n_: i_ for i_, n_ in enumerate(NAMES)}

ORDER = (
    "f0.own", "spA", "f0.fA", "f0.fB", "f0.nm", "f0.np", "f1.own", "f0.far", "spF0", "mm0", "f1.nm", "f1.np",
    "f1.far", "spF1", "mm1", "c00.own", "c01.own", "c10.own", "c00.fA", "c00.fB", "c00.nm", "c00.np",
    "r00.own", "c11.own", "r00.fA", "r00.fB", "r01.own", "c01.fA", "c01.fB", "r00.nm", "r00.np", "c01.nm",
    "c01.np", "r10.own", "c10.fA", "c10.fB", "r11.own", "c10.nm", "c10.np", "r00.far", "c00.far", "r01.fA",
    "r01.fB", "c11.fA", "c11.fB", "r01.nm", "r01.np", "c11.nm", "c11.np", "r10.fA", "r10.fB", "c01.far",
    "r10.nm", "r10.np", "c10.far", "r11.fA", "r11.fB", "c11.far", "r11.nm", "r11.np", "r01.far", "r10.far",
    "r11.far", "rf0", "rf1",
)


def split(v):
    hi = v.astype(BF16)
    return hi, (v - hi.astype(F32)).astype(BF16)


def exchange_kernel(
    a_hbm, f_hbm, dr, dc,
    abuf, ah, al, ft, fhl, pt, rb, dp, dn,
    ssem, rsem, asem, lsem, msem,
):
    row, col = lax.axis_index("row"), lax.axis_index("col")
    x_lo, z = row // 4, row % 4
    s = col // 2
    x_hi, y, core = s // 4, s % 4, col % 2

    def dev(xh, xl, yy, zz, cc):
        return (xl * 4 + zz, xh * 8 + yy * 2 + cc)

    yp, ym, y2 = (y + 1) % 4, (y + 3) % 4, (y + 2) % 4
    zp, zm, z2 = (z + 1) % 4, (z + 3) % 4, (z + 2) % 4
    d_yp, d_ym = dev(x_hi, x_lo, yp, z, core), dev(x_hi, x_lo, ym, z, core)
    d_zp, d_zm = dev(x_hi, x_lo, y, zp, core), dev(x_hi, x_lo, y, zm, core)
    d_x2 = dev(1 - x_hi, x_lo, y, z, core)
    d_xn = dev(x_hi, 1 - x_lo, y, z, core)
    d_sib = dev(x_hi, x_lo, y, z, 1 - core)
    d_tr = dev(x_lo, x_hi, (y + z) % 4, y, core)
    d_tx = dev(1 - x_lo, x_hi, (y + z) % 4, y, core)
    stays = (x_hi == x_lo) & (y == 0) & (z == 0)
    moves = jnp.logical_not(stays)
    diag = row == s

    sends, got = {}, set()

    def make(name, src, dst, to):
        i = ID[name]
        return pltpu.make_async_remote_copy(
            src_ref=src, dst_ref=dst, send_sem=ssem.at[i], recv_sem=rsem.at[i],
            device_id=to, device_id_type=MESH)

    def start(name, src, dst, to):
        sends[name] = make(name, src, dst, to)
        sends[name].start()

    def recv(name, ref):
        if name not in got:
            got.add(name)
            make(name, ref, ref, d_sib).wait_recv()

    steps = {}

    def step(name):
        def keep(f):
            steps[name] = f
        return keep

    def ring(n, slot, pos, to_up, to_down, half, own, sib=None, far=None):
        u, d, o = (pos + 1) % 4, (pos + 3) % 4, (pos + 2) % 4

        def part(i, which):
            return slot(i).at[pl.ds(which * half, half)]

        def to_sib(tag, i):
            if sib is not None:
                start(sib + tag, slot(i), slot(i), d_sib)

        def send_own(src=None):
            src = slot(pos) if src is None else src
            for m, w, to in (("pA", 0, to_up), ("mB", 1, to_down), ("pB", 1, to_up), ("mA", 0, to_down)):
                start(n + m, src.at[pl.ds(w * half, half)], part(pos, w), to)
            if sib is not None:
                start(sib + "0", src, slot(pos), d_sib)

        @step(n + ".own")
        def _():
            own(send_own)

        if far is None:
            @step(n + ".fA")
            def _():
                recv(n + "pA", part(d, 0))
                start(n + "fA", part(d, 0), part(d, 0), to_up)

            @step(n + ".fB")
            def _():
                recv(n + "mB", part(u, 1))
                start(n + "fB", part(u, 1), part(u, 1), to_down)

        @step(n + ".nm")
        def _():
            recv(n + "pA", part(d, 0))
            recv(n + "pB", part(d, 1))
            to_sib("m", d)

        @step(n + ".np")
        def _():
            recv(n + "mA", part(u, 0))
            recv(n + "mB", part(u, 1))
            to_sib("p", u)

        @step(n + ".far")
        def _():
            if far is None:
                recv(n + "fA", part(o, 0))
                recv(n + "fB", part(o, 1))
            else:
                recv(far, slot(o))
            if n == "f0":
                start("fy", slot(o), slot(o), d_x2)
            to_sib("2", o)

    def a_copy(i):
        rows = pl.ds(i * 256, 256)
        return pltpu.make_async_copy(a_hbm.at[rows], abuf.at[rows], asem.at[i])

    for i in range(8):
        a_copy(i).start()
    own_f = pltpu.make_async_copy(f_hbm, ft.at[x_hi, y, core], lsem.at[0])
    own_f.start()

    barrier = pltpu.get_barrier_semaphore()
    group = [dev(x_hi, xl, y, zz, core) for xl in (x_lo, 1 - x_lo) for zz in (z, zp, zm, z2)][1:]
    greeted = [d_yp, d_ym, d_x2, d_sib] + group
    for d in greeted:
        pl.semaphore_signal(barrier, inc=1, device_id=d, device_id_type=MESH)
    pl.semaphore_wait(barrier, len(greeted))

    def kf(t):
        return x_hi if t == 0 else 1 - x_hi

    def kr(t):
        return x_lo if t == 0 else 1 - x_lo

    def own_f0(send):
        start("fx", f_hbm, ft.at[x_hi, y, core], d_x2)
        send(f_hbm)

    def own_f1(send):
        recv("fx", ft.at[1 - x_hi, y, core])
        send()

    for t, own in enumerate((own_f0, own_f1)):
        ring(f"f{t}", lambda i, t=t: ft.at[kf(t), i, core], y, d_yp, d_ym, 8, own, f"sf{t}",
             "fy" if t == 1 else None)

    @step("spA")
    def _():
        def body(i, carry):
            a_copy(i).wait()
            rows = pl.ds(pl.multiple_of(i * 256, 256), 256)
            for xl in range(2):
                for zz in range(4):
                    r = xl * 4 + zz
                    h, l = split(abuf[rows, r * 128:(r + 1) * 128])
                    ah[zz, rows, xl * 128:(xl + 1) * 128] = h
                    al[zz, rows, xl * 128:(xl + 1) * 128] = l
            return carry
        lax.fori_loop(0, 8, body, 0)

    targets = [(xl, zz) for zz in (z2, zp, zm) for xl in (x_lo, 1 - x_lo)] + [(1 - x_lo, z)]

    def product(t, zz):
        h = kf(t)
        both = jnp.dot(fhl[...], ah[zz], preferred_element_type=F32)
        low = jnp.dot(fhl[0:128], al[zz], preferred_element_type=F32)
        p = both[:128] + (both[128:] + low)
        for xl in range(2):
            pt[t, zz, xl] = p[:, xl * 128:(xl + 1) * 128]

        @pl.when(diag)
        def _():
            for xl in range(2):
                at = pl.multiple_of(core * 1024 + (xl * 4 + zz) * 128, 128)
                pt[t, zz, xl] += ft[h, :, :, :, pl.ds(at, 128)].reshape(128, 128)

    for t in range(2):
        @step(f"spF{t}")
        def _(t=t):
            if t == 0:
                own_f.wait()
            for j, pos in (("0", y), ("m", ym), ("p", yp), ("2", y2)):
                recv(f"sf{t}{j}", ft.at[kf(t), pos, 1 - core])
            hi, lo = split(ft[kf(t)].reshape(128, 2048))
            fhl[0:128] = hi
            fhl[128:256] = lo

        @step(f"mm{t}")
        def _(t=t):
            pairs = []
            for k, (xl, zz) in enumerate(targets):
                pairs.append(make(f"p{k}{t}", pt.at[t, zz, xl], rb.at[t, k], dev(x_hi, xl, y, zz, core)))
                sends[f"p{k}{t}"] = pairs[-1]

            def body(i, carry):
                zz = jnp.where(i == 0, z2, jnp.where(i == 1, zp, jnp.where(i == 2, zm, z)))
                product(t, zz)

                for j in range(4):
                    @pl.when(i == j)
                    def _(j=j):
                        for c in pairs[2 * j:2 * j + 2]:
                            c.start()

                return carry

            lax.fori_loop(0, 4, body, 0)

        def own_c0(send, t=t):
            d = pt[t, z, x_lo]
            for k in range(7):
                recv(f"p{k}{t}", rb.at[t, k])
                d = d + rb[t, k]
            dn[t] = d.T
            if t == 1:
                start(f"sx{t}", dn.at[t], dr.at[kf(t), core, row], d_tx)

            @pl.when(moves)
            def _():
                make(f"sw{t}", dn.at[t], dr.at[kf(t), core, row], d_tr).start()

            @pl.when(stays)
            def _():
                pltpu.make_async_copy(dn.at[t], dr.at[kf(t), core, row], msem.at[t]).start()

            dp[t] = d
            start(f"cx{t}", dp.at[t], dc.at[kf(t), row], d_xn)
            send(dp.at[t])
            pltpu.make_async_copy(dp.at[t], dc.at[kf(t), row], lsem.at[1 + t]).start()

        def own_c1(send, t=t):
            recv(f"cx{t}", dc.at[kf(t), (1 - x_lo) * 4 + z])
            send()

        def own_r0(send, t=t):
            mine = dr.at[kr(t), core, x_hi * 4 + (y - z + 4) % 4]

            @pl.when(moves)
            def _():
                make(f"sw{t}", mine, mine, d_sib).wait_recv()

            @pl.when(stays)
            def _():
                pltpu.make_async_copy(dn.at[t], mine, msem.at[t]).wait()

            if t == 0:
                start(f"sx{t}", mine, mine, d_x2)
            send()

        def own_r1(send, t=t):
            recv(f"sx{t}", dr.at[kr(t), core, (1 - x_hi) * 4 + (y - z + 4) % 4])
            send()

        for j, own in enumerate((own_c0, own_c1)):
            xl = x_lo if j == 0 else 1 - x_lo
            ring(f"c{j}{t}", lambda i, t=t, xl=xl: dc.at[kf(t), xl * 4 + i], z, d_zp, d_zm, 64, own)
        for j, own in enumerate((own_r0, own_r1)):
            xh = x_hi if j == 0 else 1 - x_hi
            ring(f"r{j}{t}", lambda i, t=t, xh=xh: dr.at[kr(t), core, xh * 4 + (i - z + 4) % 4], y, d_yp, d_ym, 64, own,
                 f"{'sr' if j == 0 else 'sq'}{t}")

        @step(f"rf{t}")
        def _(t=t):
            for j in range(2):
                xh = x_hi if j == 0 else 1 - x_hi
                for tag, pos in (("0", y), ("m", ym), ("p", yp), ("2", y2)):
                    recv(f"{'sr' if j == 0 else 'sq'}{t}{tag}", dr.at[kr(t), 1 - core, xh * 4 + (pos - z + 4) % 4])

    for name in ORDER:
        steps[name]()

    for c in sends.values():
        c.wait_send()

    @pl.when(moves)
    def _():
        for t in range(2):
            make(f"sw{t}", dn.at[t], dr.at[kf(t), core, row], d_tr).wait_send()

    for t in range(2):
        pltpu.make_async_copy(dp.at[t], dc.at[kf(t), row], lsem.at[1 + t]).wait()


OUTER_ROWS = (128, 384, 512, 512, 512)


def outer_kernel(dr_ref, dc_ref, occ_ref, vir_ref, evir_ref, eocc_ref, out_hbm, ch, cl, ecol, erow, obuf, sem):
    for k in range(2):
        for r in range(8):
            h, l = split(dc_ref[k, r])
            ch[k * 128:(k + 1) * 128, r * 128:(r + 1) * 128] = h
            cl[k * 128:(k + 1) * 128, r * 128:(r + 1) * 128] = l
    row, col = lax.axis_index("row"), lax.axis_index("col")
    occ_rows, vir_rows = [], []
    for first, size in ((row * 16, 16), (col * 8, 8)):
        at = pl.ds(pl.multiple_of(first, 8), size)
        occ_rows.append(occ_ref[at])
        vir_rows.append(vir_ref[at])
    occ = jnp.concatenate(occ_rows, axis=0)
    vir = jnp.concatenate(vir_rows, axis=0)
    low, high = vir & 127, vir >> 7
    picked = jnp.zeros((24, 128), F32)
    for h in range(16):
        table = jnp.broadcast_to(evir_ref[h:h + 1], (24, 128))
        got = jnp.take_along_axis(table, low, axis=1, mode="promise_in_bounds")
        picked = jnp.where(high == h, got, picked)
    taken = jnp.zeros((24, 128), F32)
    for o in range(64):
        taken = jnp.where(occ == o, eocc_ref[o], taken)
    negative = taken - picked
    erow[...] = negative[16:24]
    for i in range(16):
        ecol[i * 128:(i + 1) * 128] = jnp.broadcast_to(negative[i:i + 1], (128, 128)).T

    copies = []
    first = 0
    for i, size in enumerate(OUTER_ROWS):
        rows = slice(first, first + size)
        x = jnp.concatenate([dr_ref[0, rows], dr_ref[1, rows]], axis=1)
        h, l = split(x)
        acc = jnp.dot(h, ch[...], preferred_element_type=F32)
        acc += jnp.dot(l, ch[...], preferred_element_type=F32)
        acc += jnp.dot(h, cl[...], preferred_element_type=F32)
        e = ecol[rows]
        for n in range(8):
            lanes = slice(n * 128, (n + 1) * 128)
            obuf[rows, lanes] = acc[:, lanes] / (e + erow[n:n + 1])
        copies.append(pltpu.make_async_copy(obuf.at[rows], out_hbm.at[rows], sem.at[i]))
        copies[-1].start()
        first += size
    for c in copies:
        c.wait()


def local(amplitudes, factors, occ_index, vir_index, occ_energy, vir_energy):
    hbm = pl.BlockSpec(memory_space=pl.ANY)
    vmem = lambda *shape: pltpu.VMEM(shape, F32)
    dr, dc = pl.pallas_call(
        exchange_kernel,
        out_shape=(
            jax.ShapeDtypeStruct((2, 2, 8, 128, 128), F32),
            jax.ShapeDtypeStruct((2, 8, 128, 128), F32),
        ),
        in_specs=[hbm, pl.BlockSpec(memory_space=pltpu.HBM)],
        out_specs=(hbm, hbm),
        scratch_shapes=[
            vmem(2048, 1024),
            pltpu.VMEM((4, 2048, 256), BF16),
            pltpu.VMEM((4, 2048, 256), BF16),
            vmem(2, 4, 2, 16, 2048),
            pltpu.VMEM((256, 2048), BF16),
            vmem(2, 4, 2, 128, 128),
            vmem(2, 7, 128, 128),
            vmem(2, 128, 128),
            vmem(2, 128, 128),
            pltpu.SemaphoreType.DMA((len(NAMES),)),
            pltpu.SemaphoreType.DMA((len(NAMES),)),
            pltpu.SemaphoreType.DMA((8,)),
            pltpu.SemaphoreType.DMA((3,)),
            pltpu.SemaphoreType.DMA((2,)),
        ],
        compiler_params=pltpu.CompilerParams(
            collective_id=0, has_side_effects=True, vmem_limit_bytes=48 * 1024 * 1024),
        name="exchange",
    )(amplitudes, pltpu.with_memory_space_constraint(factors.T, pltpu.HBM))
    in_vmem = pl.BlockSpec(memory_space=pltpu.VMEM)
    return pl.pallas_call(
        outer_kernel,
        out_shape=jax.ShapeDtypeStruct((2048, 1024), F32),
        in_specs=[in_vmem] * 5 + [pl.BlockSpec(memory_space=pltpu.SMEM)],
        out_specs=hbm,
        scratch_shapes=[
            pltpu.VMEM((256, 1024), BF16),
            pltpu.VMEM((256, 1024), BF16),
            vmem(2048, 128),
            vmem(8, 128),
            vmem(2048, 1024),
            pltpu.SemaphoreType.DMA((len(OUTER_ROWS),)),
        ],
        compiler_params=pltpu.CompilerParams(vmem_limit_bytes=32 * 1024 * 1024),
        name="outer",
    )(
        dr.reshape(2, 2048, 128), dc, occ_index.reshape(128, 128), vir_index.reshape(128, 128),
        vir_energy.reshape(16, 128), occ_energy,
    )


def solution(mesh):
    return jax.shard_map(
        local,
        mesh=mesh,
        in_specs=(P("row", "col"), P("row", "col"), P(), P(), P(), P()),
        out_specs=P("row", "col"),
        check_vma=False,
    )
```

```python
import functools

import jax
import jax.numpy as jnp
from jax import lax
from jax.experimental import pallas as pl
from jax.experimental.pallas import tpu as pltpu
from jax.sharding import PartitionSpec as P

MESH = pl.DeviceIdType.MESH
F32 = jnp.float32
BF16 = jnp.bfloat16
RING = ("pA", "mB", "pB", "mA", "fA", "fB")
NAMES = ["fx", "fy"]
for t_ in range(2):
    for r_ in ("f0", "f1"):
        NAMES += [f"{r_}{m_}" for m_ in RING if t_ == 0 and (r_ == "f0" or m_[0] != "f")]
    for r_ in ("c0", "c1", "r0", "r1"):
        NAMES += [f"{r_}{t_}{m_}" for m_ in RING]
    NAMES += [f"{q_}{t_}{j_}" for q_ in ("sf", "sr", "sq") for j_ in ("0", "m", "p", "2")]
    NAMES += [f"{m_}{t_}" for m_ in ("p0", "p1", "p2", "p3", "p4", "p5", "p6", "cx", "sw", "sx")]
ID = {n_: i_ for i_, n_ in enumerate(NAMES)}

ORDER = (
    "f0.own", "spA", "f0.fA", "f0.fB", "f0.nm", "f0.np", "f1.own", "f0.far", "spF0", "mm0a", "f1.nm", "f1.np",
    "mm0b", "f1.far", "spF1", "mm1", "c00.own", "c01.own", "c10.own", "c00.fA", "c00.fB", "c00.nm", "c00.np",
    "r00.own", "c11.own", "r00.fA", "r00.fB", "r01.own", "c01.fA", "c01.fB", "r00.nm", "r00.np", "c01.nm",
    "c01.np", "r10.own", "c10.fA", "c10.fB", "r11.own", "c10.nm", "c10.np", "r00.far", "c00.far", "r01.fA",
    "r01.fB", "c11.fA", "c11.fB", "r01.nm", "r01.np", "c11.nm", "c11.np", "r10.fA", "r10.fB", "c01.far",
    "r10.nm", "r10.np", "c10.far", "r11.fA", "r11.fB", "c11.far", "r11.nm", "r11.np", "r01.far", "r10.far",
    "r11.far", "rf0", "rf1",
)


def split(v):
    hi = v.astype(BF16)
    return hi, (v - hi.astype(F32)).astype(BF16)


def exchange_kernel(
    a_hbm, f_hbm, dr, dc,
    abuf, ah, al, ft, fhl, pt, rb, dp, dn,
    ssem, rsem, asem, lsem, msem,
):
    row, col = lax.axis_index("row"), lax.axis_index("col")
    x_lo, z = row // 4, row % 4
    s = col // 2
    x_hi, y, core = s // 4, s % 4, col % 2

    def dev(xh, xl, yy, zz, cc):
        return (xl * 4 + zz, xh * 8 + yy * 2 + cc)

    yp, ym, y2 = (y + 1) % 4, (y + 3) % 4, (y + 2) % 4
    zp, zm, z2 = (z + 1) % 4, (z + 3) % 4, (z + 2) % 4
    d_yp, d_ym = dev(x_hi, x_lo, yp, z, core), dev(x_hi, x_lo, ym, z, core)
    d_zp, d_zm = dev(x_hi, x_lo, y, zp, core), dev(x_hi, x_lo, y, zm, core)
    d_x2 = dev(1 - x_hi, x_lo, y, z, core)
    d_xn = dev(x_hi, 1 - x_lo, y, z, core)
    d_sib = dev(x_hi, x_lo, y, z, 1 - core)
    d_tr = dev(x_lo, x_hi, (y + z) % 4, y, core)
    d_tx = dev(1 - x_lo, x_hi, (y + z) % 4, y, core)
    stays = (x_hi == x_lo) & (y == 0) & (z == 0)
    moves = jnp.logical_not(stays)
    diag = row == s

    sends, got = {}, set()

    def make(name, src, dst, to):
        i = ID[name]
        return pltpu.make_async_remote_copy(
            src_ref=src, dst_ref=dst, send_sem=ssem.at[i], recv_sem=rsem.at[i],
            device_id=to, device_id_type=MESH)

    def start(name, src, dst, to):
        sends[name] = make(name, src, dst, to)
        sends[name].start()

    def recv(name, ref):
        if name not in got:
            got.add(name)
            make(name, ref, ref, d_sib).wait_recv()

    steps = {}

    def step(name):
        def keep(f):
            steps[name] = f
        return keep

    def ring(n, slot, pos, to_up, to_down, half, own, sib=None, far=None):
        u, d, o = (pos + 1) % 4, (pos + 3) % 4, (pos + 2) % 4

        def part(i, which):
            return slot(i).at[pl.ds(which * half, half)]

        def to_sib(tag, i):
            if sib is not None:
                start(sib + tag, slot(i), slot(i), d_sib)

        def send_own(src=None):
            src = slot(pos) if src is None else src
            for m, w, to in (("pA", 0, to_up), ("mB", 1, to_down), ("pB", 1, to_up), ("mA", 0, to_down)):
                start(n + m, src.at[pl.ds(w * half, half)], part(pos, w), to)
            if sib is not None:
                start(sib + "0", src, slot(pos), d_sib)

        @step(n + ".own")
        def _():
            own(send_own)

        if far is None:
            @step(n + ".fA")
            def _():
                recv(n + "pA", part(d, 0))
                start(n + "fA", part(d, 0), part(d, 0), to_up)

            @step(n + ".fB")
            def _():
                recv(n + "mB", part(u, 1))
                start(n + "fB", part(u, 1), part(u, 1), to_down)

        @step(n + ".nm")
        def _():
            recv(n + "pA", part(d, 0))
            recv(n + "pB", part(d, 1))
            to_sib("m", d)

        @step(n + ".np")
        def _():
            recv(n + "mA", part(u, 0))
            recv(n + "mB", part(u, 1))
            to_sib("p", u)

        @step(n + ".far")
        def _():
            if far is None:
                recv(n + "fA", part(o, 0))
                recv(n + "fB", part(o, 1))
            else:
                recv(far, slot(o))
            if n == "f0":
                start("fy", slot(o), slot(o), d_x2)
            to_sib("2", o)

    def a_copy(i):
        rows = pl.ds(i * 256, 256)
        return pltpu.make_async_copy(a_hbm.at[rows], abuf.at[rows], asem.at[i])

    for i in range(8):
        a_copy(i).start()
    own_f = pltpu.make_async_copy(f_hbm, ft.at[x_hi, y, core], lsem.at[0])
    own_f.start()

    barrier = pltpu.get_barrier_semaphore()
    group = [dev(x_hi, xl, y, zz, core) for xl in (x_lo, 1 - x_lo) for zz in (z, zp, zm, z2)][1:]
    greeted = [d_yp, d_ym, d_x2, d_sib] + group
    for d in greeted:
        pl.semaphore_signal(barrier, inc=1, device_id=d, device_id_type=MESH)
    pl.semaphore_wait(barrier, len(greeted))

    def kf(t):
        return x_hi if t == 0 else 1 - x_hi

    def kr(t):
        return x_lo if t == 0 else 1 - x_lo

    def own_f0(send):
        start("fx", f_hbm, ft.at[x_hi, y, core], d_x2)
        send(f_hbm)

    def own_f1(send):
        recv("fx", ft.at[1 - x_hi, y, core])
        send()

    for t, own in enumerate((own_f0, own_f1)):
        ring(f"f{t}", lambda i, t=t: ft.at[kf(t), i, core], y, d_yp, d_ym, 8, own, f"sf{t}",
             "fy" if t == 1 else None)

    @step("spA")
    def _():
        def body(i, carry):
            a_copy(i).wait()
            rows = pl.ds(pl.multiple_of(i * 256, 256), 256)
            for xl in range(2):
                for zz in range(4):
                    r = xl * 4 + zz
                    h, l = split(abuf[rows, r * 128:(r + 1) * 128])
                    ah[zz, rows, xl * 128:(xl + 1) * 128] = h
                    al[zz, rows, xl * 128:(xl + 1) * 128] = l
            return carry
        lax.fori_loop(0, 8, body, 0)

    targets = [(xl, zz) for zz in (z2, zp, zm) for xl in (x_lo, 1 - x_lo)] + [(1 - x_lo, z)]

    def product(t, zz):
        h = kf(t)
        both = jnp.dot(fhl[...], ah[zz], preferred_element_type=F32)
        low = jnp.dot(fhl[0:128], al[zz], preferred_element_type=F32)
        p = both[:128] + (both[128:] + low)
        for xl in range(2):
            pt[t, zz, xl] = p[:, xl * 128:(xl + 1) * 128]

        @pl.when(diag)
        def _():
            for xl in range(2):
                at = pl.multiple_of(core * 1024 + (xl * 4 + zz) * 128, 128)
                pt[t, zz, xl] += ft[h, :, :, :, pl.ds(at, 128)].reshape(128, 128)

    for t in range(2):
        @step(f"spF{t}")
        def _(t=t):
            if t == 0:
                own_f.wait()
            for j, pos in (("0", y), ("m", ym), ("p", yp), ("2", y2)):
                recv(f"sf{t}{j}", ft.at[kf(t), pos, 1 - core])
            hi, lo = split(ft[kf(t)].reshape(128, 2048))
            fhl[0:128] = hi
            fhl[128:256] = lo

        pairs_of = {}

        def products(t, lo, hi, pairs_of=pairs_of):
            if lo == 0:
                pairs_of[t] = []
                for k, (xl, zz) in enumerate(targets):
                    to = dev(x_hi, xl, y, zz, core)
                    pairs_of[t].append(make(f"p{k}{t}", pt.at[t, zz, xl], rb.at[t, k], to))
                    sends[f"p{k}{t}"] = pairs_of[t][-1]
            pairs = pairs_of[t]

            def body(i, carry):
                zz = jnp.where(i == 0, z2, jnp.where(i == 1, zp, jnp.where(i == 2, zm, z)))
                product(t, zz)

                for j in range(4):
                    @pl.when(i == j)
                    def _(j=j):
                        for c in pairs[2 * j:2 * j + 2]:
                            c.start()

                return carry

            lax.fori_loop(lo, hi, body, 0)

        cuts = (0, 2, 4) if t == 0 else (0, 4)
        for j in range(len(cuts) - 1):
            @step(f"mm{t}" + ("ab"[j] if t == 0 else ""))
            def _(t=t, lo=cuts[j], hi=cuts[j + 1], products=products):
                products(t, lo, hi)

        def own_c0(send, t=t):
            d = pt[t, z, x_lo]
            for k in range(7):
                recv(f"p{k}{t}", rb.at[t, k])
                d = d + rb[t, k]
            dn[t] = d.T
            if t == 1:
                start(f"sx{t}", dn.at[t], dr.at[kf(t), core, row], d_tx)

            @pl.when(moves)
            def _():
                make(f"sw{t}", dn.at[t], dr.at[kf(t), core, row], d_tr).start()

            @pl.when(stays)
            def _():
                pltpu.make_async_copy(dn.at[t], dr.at[kf(t), core, row], msem.at[t]).start()

            dp[t] = d
            start(f"cx{t}", dp.at[t], dc.at[kf(t), row], d_xn)
            send(dp.at[t])
            pltpu.make_async_copy(dp.at[t], dc.at[kf(t), row], lsem.at[1 + t]).start()

        def own_c1(send, t=t):
            recv(f"cx{t}", dc.at[kf(t), (1 - x_lo) * 4 + z])
            send()

        def own_r0(send, t=t):
            mine = dr.at[kr(t), core, x_hi * 4 + (y - z + 4) % 4]

            @pl.when(moves)
            def _():
                make(f"sw{t}", mine, mine, d_sib).wait_recv()

            @pl.when(stays)
            def _():
                pltpu.make_async_copy(dn.at[t], mine, msem.at[t]).wait()

            if t == 0:
                start(f"sx{t}", mine, mine, d_x2)
            send()

        def own_r1(send, t=t):
            recv(f"sx{t}", dr.at[kr(t), core, (1 - x_hi) * 4 + (y - z + 4) % 4])
            send()

        for j, own in enumerate((own_c0, own_c1)):
            xl = x_lo if j == 0 else 1 - x_lo
            ring(f"c{j}{t}", lambda i, t=t, xl=xl: dc.at[kf(t), xl * 4 + i], z, d_zp, d_zm, 64, own)
        for j, own in enumerate((own_r0, own_r1)):
            xh = x_hi if j == 0 else 1 - x_hi
            ring(f"r{j}{t}", lambda i, t=t, xh=xh: dr.at[kr(t), core, xh * 4 + (i - z + 4) % 4], y, d_yp, d_ym, 64, own,
                 f"{'sr' if j == 0 else 'sq'}{t}")

        @step(f"rf{t}")
        def _(t=t):
            for j in range(2):
                xh = x_hi if j == 0 else 1 - x_hi
                for tag, pos in (("0", y), ("m", ym), ("p", yp), ("2", y2)):
                    recv(f"{'sr' if j == 0 else 'sq'}{t}{tag}", dr.at[kr(t), 1 - core, xh * 4 + (pos - z + 4) % 4])

    for name in ORDER:
        steps[name]()

    for c in sends.values():
        c.wait_send()

    @pl.when(moves)
    def _():
        for t in range(2):
            make(f"sw{t}", dn.at[t], dr.at[kf(t), core, row], d_tr).wait_send()

    for t in range(2):
        pltpu.make_async_copy(dp.at[t], dc.at[kf(t), row], lsem.at[1 + t]).wait()


OUTER_ROWS = (512, 512, 512, 384, 128)


def outer_kernel(dr_ref, dc_ref, occ_ref, vir_ref, evir_ref, eocc_ref, out_hbm, ch, cl, ecol, erow, obuf, sem):
    for k in range(2):
        for r in range(8):
            h, l = split(dc_ref[k, r])
            ch[k * 128:(k + 1) * 128, r * 128:(r + 1) * 128] = h
            cl[k * 128:(k + 1) * 128, r * 128:(r + 1) * 128] = l
    row, col = lax.axis_index("row"), lax.axis_index("col")
    occ_rows, vir_rows = [], []
    for first, size in ((row * 16, 16), (col * 8, 8)):
        at = pl.ds(pl.multiple_of(first, 8), size)
        occ_rows.append(occ_ref[at])
        vir_rows.append(vir_ref[at])
    occ = jnp.concatenate(occ_rows, axis=0)
    vir = jnp.concatenate(vir_rows, axis=0)
    low, high = vir & 127, vir >> 7
    picked = jnp.zeros((24, 128), F32)
    for h in range(16):
        table = jnp.broadcast_to(evir_ref[h:h + 1], (24, 128))
        got = jnp.take_along_axis(table, low, axis=1, mode="promise_in_bounds")
        picked = jnp.where(high == h, got, picked)
    taken = jnp.zeros((24, 128), F32)
    for o in range(64):
        taken = jnp.where(occ == o, eocc_ref[o], taken)
    negative = taken - picked
    erow[...] = negative[16:24]
    for i in range(16):
        ecol[i * 128:(i + 1) * 128] = jnp.broadcast_to(negative[i:i + 1], (128, 128)).T

    copies = []
    first = 0
    for i, size in enumerate(OUTER_ROWS):
        rows = slice(first, first + size)
        x = jnp.concatenate([dr_ref[0, rows], dr_ref[1, rows]], axis=1)
        h, l = split(x)
        acc = jnp.dot(h, ch[...], preferred_element_type=F32)
        acc += jnp.dot(l, ch[...], preferred_element_type=F32)
        acc += jnp.dot(h, cl[...], preferred_element_type=F32)
        e = ecol[rows]
        for n in range(8):
            lanes = slice(n * 128, (n + 1) * 128)
            obuf[rows, lanes] = acc[:, lanes] / (e + erow[n:n + 1])
        copies.append(pltpu.make_async_copy(obuf.at[rows], out_hbm.at[rows], sem.at[i]))
        copies[-1].start()
        first += size
    for c in copies:
        c.wait()


def local(amplitudes, factors, occ_index, vir_index, occ_energy, vir_energy):
    hbm = pl.BlockSpec(memory_space=pl.ANY)
    vmem = lambda *shape: pltpu.VMEM(shape, F32)
    dr, dc = pl.pallas_call(
        exchange_kernel,
        out_shape=(
            jax.ShapeDtypeStruct((2, 2, 8, 128, 128), F32),
            jax.ShapeDtypeStruct((2, 8, 128, 128), F32),
        ),
        in_specs=[hbm, pl.BlockSpec(memory_space=pltpu.HBM)],
        out_specs=(hbm, hbm),
        scratch_shapes=[
            vmem(2048, 1024),
            pltpu.VMEM((4, 2048, 256), BF16),
            pltpu.VMEM((4, 2048, 256), BF16),
            vmem(2, 4, 2, 16, 2048),
            pltpu.VMEM((256, 2048), BF16),
            vmem(2, 4, 2, 128, 128),
            vmem(2, 7, 128, 128),
            vmem(2, 128, 128),
            vmem(2, 128, 128),
            pltpu.SemaphoreType.DMA((len(NAMES),)),
            pltpu.SemaphoreType.DMA((len(NAMES),)),
            pltpu.SemaphoreType.DMA((8,)),
            pltpu.SemaphoreType.DMA((3,)),
            pltpu.SemaphoreType.DMA((2,)),
        ],
        compiler_params=pltpu.CompilerParams(
            collective_id=0, has_side_effects=True, vmem_limit_bytes=48 * 1024 * 1024),
        name="exchange",
    )(amplitudes, pltpu.with_memory_space_constraint(factors.T, pltpu.HBM))
    in_vmem = pl.BlockSpec(memory_space=pltpu.VMEM)
    return pl.pallas_call(
        outer_kernel,
        out_shape=jax.ShapeDtypeStruct((2048, 1024), F32),
        in_specs=[in_vmem] * 5 + [pl.BlockSpec(memory_space=pltpu.SMEM)],
        out_specs=hbm,
        scratch_shapes=[
            pltpu.VMEM((256, 1024), BF16),
            pltpu.VMEM((256, 1024), BF16),
            vmem(2048, 128),
            vmem(8, 128),
            vmem(2048, 1024),
            pltpu.SemaphoreType.DMA((len(OUTER_ROWS),)),
        ],
        compiler_params=pltpu.CompilerParams(vmem_limit_bytes=32 * 1024 * 1024),
        name="outer",
    )(
        dr.reshape(2, 2048, 128), dc, occ_index.reshape(128, 128), vir_index.reshape(128, 128),
        vir_energy.reshape(16, 128), occ_energy,
    )


def solution(mesh):
    return jax.shard_map(
        local,
        mesh=mesh,
        in_specs=(P("row", "col"), P("row", "col"), P(), P(), P(), P()),
        out_specs=P("row", "col"),
        check_vma=False,
    )
```

```python
import functools

import jax
import jax.numpy as jnp
from jax import lax
from jax.experimental import pallas as pl
from jax.experimental.pallas import tpu as pltpu
from jax.sharding import PartitionSpec as P

MESH = pl.DeviceIdType.MESH
F32 = jnp.float32
BF16 = jnp.bfloat16
RING = ("pA", "mB", "pB", "mA", "fA", "fB")
NAMES = ["fx", "fy"]
for t_ in range(2):
    for r_ in ("f0", "f1"):
        NAMES += [f"{r_}{m_}" for m_ in RING if t_ == 0 and (r_ == "f0" or m_[0] != "f")]
    for r_ in ("c0", "c1", "r0", "r1"):
        NAMES += [f"{r_}{t_}{m_}" for m_ in RING]
    NAMES += [f"{q_}{t_}{j_}" for q_ in ("sf", "sr", "sq") for j_ in ("0", "m", "p", "2")]
    NAMES += [f"{m_}{t_}" for m_ in ("p0", "p1", "p2", "p3", "p4", "p5", "p6", "cx", "sw", "sx")]
ID = {n_: i_ for i_, n_ in enumerate(NAMES)}

ORDER = (
    "f0.own", "spA", "f0.fA", "f0.fB", "f0.nm", "f0.np", "f1.own", "f0.far", "spF0", "mm0a", "f1.nm", "f1.np",
    "mm0b", "f1.far", "spF1", "mm1", "c00.own", "c01.own", "c10.own", "c00.fA", "c00.fB", "c00.nm", "c00.np",
    "r00.own", "c11.own", "r00.fA", "r00.fB", "r01.own", "c01.fA", "c01.fB", "r00.nm", "r00.np", "c01.nm",
    "c01.np", "r10.own", "c10.fA", "c10.fB", "r11.own", "c10.nm", "c10.np", "r00.far", "c00.far", "r01.fA",
    "r01.fB", "c11.fA", "c11.fB", "r01.nm", "r01.np", "c11.nm", "c11.np", "r10.fA", "r10.fB", "c01.far",
    "r10.nm", "r10.np", "c10.far", "r11.fA", "r11.fB", "c11.far", "r11.nm", "r11.np", "r01.far", "r10.far",
    "r11.far", "rf0", "rf1",
)


def split(v):
    hi = v.astype(BF16)
    return hi, (v - hi.astype(F32)).astype(BF16)


def exchange_kernel(
    a_hbm, f_hbm, dr, dc,
    abuf, ah, al, ft, fhl, pt, rb, dp, dn,
    ssem, rsem, asem, lsem, msem,
):
    row, col = lax.axis_index("row"), lax.axis_index("col")
    x_lo, z = row // 4, row % 4
    s = col // 2
    x_hi, y, core = s // 4, s % 4, col % 2

    def dev(xh, xl, yy, zz, cc):
        return (xl * 4 + zz, xh * 8 + yy * 2 + cc)

    yp, ym, y2 = (y + 1) % 4, (y + 3) % 4, (y + 2) % 4
    zp, zm, z2 = (z + 1) % 4, (z + 3) % 4, (z + 2) % 4
    d_yp, d_ym = dev(x_hi, x_lo, yp, z, core), dev(x_hi, x_lo, ym, z, core)
    d_zp, d_zm = dev(x_hi, x_lo, y, zp, core), dev(x_hi, x_lo, y, zm, core)
    d_x2 = dev(1 - x_hi, x_lo, y, z, core)
    d_xn = dev(x_hi, 1 - x_lo, y, z, core)
    d_sib = dev(x_hi, x_lo, y, z, 1 - core)
    d_tr = dev(x_lo, x_hi, (y + z) % 4, y, core)
    d_tx = dev(1 - x_lo, x_hi, (y + z) % 4, y, core)
    stays = (x_hi == x_lo) & (y == 0) & (z == 0)
    moves = jnp.logical_not(stays)
    diag = row == s

    sends, got = {}, set()

    def make(name, src, dst, to):
        i = ID[name]
        return pltpu.make_async_remote_copy(
            src_ref=src, dst_ref=dst, send_sem=ssem.at[i], recv_sem=rsem.at[i],
            device_id=to, device_id_type=MESH)

    def start(name, src, dst, to):
        sends[name] = make(name, src, dst, to)
        sends[name].start()

    def recv(name, ref):
        if name not in got:
            got.add(name)
            make(name, ref, ref, d_sib).wait_recv()

    steps = {}

    def step(name):
        def keep(f):
            steps[name] = f
        return keep

    def ring(n, slot, pos, to_up, to_down, half, own, sib=None, far=None):
        u, d, o = (pos + 1) % 4, (pos + 3) % 4, (pos + 2) % 4

        def part(i, which):
            return slot(i).at[pl.ds(which * half, half)]

        def to_sib(tag, i):
            if sib is not None:
                start(sib + tag, slot(i), slot(i), d_sib)

        def send_own(src=None):
            src = slot(pos) if src is None else src
            for m, w, to in (("pA", 0, to_up), ("mB", 1, to_down), ("pB", 1, to_up), ("mA", 0, to_down)):
                start(n + m, src.at[pl.ds(w * half, half)], part(pos, w), to)
            if sib is not None:
                start(sib + "0", src, slot(pos), d_sib)

        @step(n + ".own")
        def _():
            own(send_own)

        if far is None:
            @step(n + ".fA")
            def _():
                recv(n + "pA", part(d, 0))
                start(n + "fA", part(d, 0), part(d, 0), to_up)

            @step(n + ".fB")
            def _():
                recv(n + "mB", part(u, 1))
                start(n + "fB", part(u, 1), part(u, 1), to_down)

        @step(n + ".nm")
        def _():
            recv(n + "pA", part(d, 0))
            recv(n + "pB", part(d, 1))
            to_sib("m", d)

        @step(n + ".np")
        def _():
            recv(n + "mA", part(u, 0))
            recv(n + "mB", part(u, 1))
            to_sib("p", u)

        @step(n + ".far")
        def _():
            if far is None:
                recv(n + "fA", part(o, 0))
                recv(n + "fB", part(o, 1))
            else:
                recv(far, slot(o))
            if n == "f0":
                start("fy", slot(o), slot(o), d_x2)
            to_sib("2", o)

    def a_copy(i):
        rows = pl.ds(i * 256, 256)
        return pltpu.make_async_copy(a_hbm.at[rows], abuf.at[rows], asem.at[i])

    for i in range(8):
        a_copy(i).start()
    own_f = pltpu.make_async_copy(f_hbm, ft.at[x_hi, y, core], lsem.at[0])
    own_f.start()

    barrier = pltpu.get_barrier_semaphore()
    group = [dev(x_hi, xl, y, zz, core) for xl in (x_lo, 1 - x_lo) for zz in (z, zp, zm, z2)][1:]
    greeted = [d_yp, d_ym, d_x2, d_sib] + group
    for d in greeted:
        pl.semaphore_signal(barrier, inc=1, device_id=d, device_id_type=MESH)
    pl.semaphore_wait(barrier, len(greeted))

    def kf(t):
        return x_hi if t == 0 else 1 - x_hi

    def kr(t):
        return x_lo if t == 0 else 1 - x_lo

    def own_f0(send):
        start("fx", f_hbm, ft.at[x_hi, y, core], d_x2)
        send(f_hbm)

    def own_f1(send):
        recv("fx", ft.at[1 - x_hi, y, core])
        send()

    for t, own in enumerate((own_f0, own_f1)):
        ring(f"f{t}", lambda i, t=t: ft.at[kf(t), i, core], y, d_yp, d_ym, 8, own, f"sf{t}",
             "fy" if t == 1 else None)

    @step("spA")
    def _():
        def body(i, carry):
            a_copy(i).wait()
            rows = pl.ds(pl.multiple_of(i * 256, 256), 256)
            for xl in range(2):
                for zz in range(4):
                    r = xl * 4 + zz
                    h, l = split(abuf[rows, r * 128:(r + 1) * 128])
                    ah[zz, rows, xl * 128:(xl + 1) * 128] = h
                    al[zz, rows, xl * 128:(xl + 1) * 128] = l
            return carry
        lax.fori_loop(0, 8, body, 0)

    targets = [(xl, zz) for zz in (z2, zp, zm) for xl in (x_lo, 1 - x_lo)] + [(1 - x_lo, z)]

    def product(t, zz):
        h = kf(t)
        both = jnp.dot(fhl[...], ah[zz], preferred_element_type=F32)
        low = jnp.dot(fhl[0:128], al[zz], preferred_element_type=F32)
        p = both[:128] + (both[128:] + low)
        for xl in range(2):
            pt[t, zz, xl] = p[:, xl * 128:(xl + 1) * 128]

        @pl.when(diag)
        def _():
            for xl in range(2):
                at = pl.multiple_of(core * 1024 + (xl * 4 + zz) * 128, 128)
                pt[t, zz, xl] += ft[h, :, :, :, pl.ds(at, 128)].reshape(128, 128)

    for t in range(2):
        @step(f"spF{t}")
        def _(t=t):
            if t == 0:
                own_f.wait()
            for j, pos in (("0", y), ("m", ym), ("p", yp), ("2", y2)):
                recv(f"sf{t}{j}", ft.at[kf(t), pos, 1 - core])
            hi, lo = split(ft[kf(t)].reshape(128, 2048))
            fhl[0:128] = hi
            fhl[128:256] = lo

        pairs_of = {}

        def products(t, lo, hi, pairs_of=pairs_of):
            if lo == 0:
                pairs_of[t] = []
                for k, (xl, zz) in enumerate(targets):
                    to = dev(x_hi, xl, y, zz, core)
                    pairs_of[t].append(make(f"p{k}{t}", pt.at[t, zz, xl], rb.at[t, k], to))
                    sends[f"p{k}{t}"] = pairs_of[t][-1]
            pairs = pairs_of[t]

            def body(i, carry):
                zz = jnp.where(i == 0, z2, jnp.where(i == 1, zp, jnp.where(i == 2, zm, z)))
                product(t, zz)

                for j in range(4):
                    @pl.when(i == j)
                    def _(j=j):
                        for c in pairs[2 * j:2 * j + 2]:
                            c.start()

                return carry

            lax.fori_loop(lo, hi, body, 0)

        cuts = (0, 2, 4) if t == 0 else (0, 4)
        for j in range(len(cuts) - 1):
            @step(f"mm{t}" + ("ab"[j] if t == 0 else ""))
            def _(t=t, lo=cuts[j], hi=cuts[j + 1], products=products):
                products(t, lo, hi)

        def own_c0(send, t=t):
            d = pt[t, z, x_lo]
            for k in range(7):
                recv(f"p{k}{t}", rb.at[t, k])
                d = d + rb[t, k]
            dn[t] = d.T
            if t == 1:
                start(f"sx{t}", dn.at[t], dr.at[kf(t), core, row], d_tx)

            @pl.when(moves)
            def _():
                make(f"sw{t}", dn.at[t], dr.at[kf(t), core, row], d_tr).start()

            @pl.when(stays)
            def _():
                pltpu.make_async_copy(dn.at[t], dr.at[kf(t), core, row], msem.at[t]).start()

            dp[t] = d
            start(f"cx{t}", dp.at[t], dc.at[kf(t), row], d_xn)
            send(dp.at[t])
            pltpu.make_async_copy(dp.at[t], dc.at[kf(t), row], lsem.at[1 + t]).start()

        def own_c1(send, t=t):
            recv(f"cx{t}", dc.at[kf(t), (1 - x_lo) * 4 + z])
            send()

        def own_r0(send, t=t):
            mine = dr.at[kr(t), core, x_hi * 4 + (y - z + 4) % 4]

            @pl.when(moves)
            def _():
                make(f"sw{t}", mine, mine, d_sib).wait_recv()

            @pl.when(stays)
            def _():
                pltpu.make_async_copy(dn.at[t], mine, msem.at[t]).wait()

            if t == 0:
                start(f"sx{t}", mine, mine, d_x2)
            send()

        def own_r1(send, t=t):
            recv(f"sx{t}", dr.at[kr(t), core, (1 - x_hi) * 4 + (y - z + 4) % 4])
            send()

        for j, own in enumerate((own_c0, own_c1)):
            xl = x_lo if j == 0 else 1 - x_lo
            ring(f"c{j}{t}", lambda i, t=t, xl=xl: dc.at[kf(t), xl * 4 + i], z, d_zp, d_zm, 64, own)
        for j, own in enumerate((own_r0, own_r1)):
            xh = x_hi if j == 0 else 1 - x_hi
            ring(f"r{j}{t}", lambda i, t=t, xh=xh: dr.at[kr(t), core, xh * 4 + (i - z + 4) % 4], y, d_yp, d_ym, 64, own,
                 f"{'sr' if j == 0 else 'sq'}{t}")

        @step(f"rf{t}")
        def _(t=t):
            for j in range(2):
                xh = x_hi if j == 0 else 1 - x_hi
                for tag, pos in (("0", y), ("m", ym), ("p", yp), ("2", y2)):
                    recv(f"{'sr' if j == 0 else 'sq'}{t}{tag}", dr.at[kr(t), 1 - core, xh * 4 + (pos - z + 4) % 4])

    for name in ORDER:
        steps[name]()

    for c in sends.values():
        c.wait_send()

    @pl.when(moves)
    def _():
        for t in range(2):
            make(f"sw{t}", dn.at[t], dr.at[kf(t), core, row], d_tr).wait_send()

    for t in range(2):
        pltpu.make_async_copy(dp.at[t], dc.at[kf(t), row], lsem.at[1 + t]).wait()


OUTER_ROWS = (768, 640, 512, 128)


def outer_kernel(dr_ref, dc_ref, occ_ref, vir_ref, evir_ref, eocc_ref, out_hbm, ch, cl, ecol, erow, obuf, sem):
    for k in range(2):
        for r in range(8):
            h, l = split(dc_ref[k, r])
            ch[k * 128:(k + 1) * 128, r * 128:(r + 1) * 128] = h
            cl[k * 128:(k + 1) * 128, r * 128:(r + 1) * 128] = l
    row, col = lax.axis_index("row"), lax.axis_index("col")
    occ_rows, vir_rows = [], []
    for first, size in ((row * 16, 16), (col * 8, 8)):
        at = pl.ds(pl.multiple_of(first, 8), size)
        occ_rows.append(occ_ref[at])
        vir_rows.append(vir_ref[at])
    occ = jnp.concatenate(occ_rows, axis=0)
    vir = jnp.concatenate(vir_rows, axis=0)
    low, high = vir & 127, vir >> 7
    picked = jnp.zeros((24, 128), F32)
    for h in range(16):
        table = jnp.broadcast_to(evir_ref[h:h + 1], (24, 128))
        got = jnp.take_along_axis(table, low, axis=1, mode="promise_in_bounds")
        picked = jnp.where(high == h, got, picked)
    taken = jnp.zeros((24, 128), F32)
    for o in range(64):
        taken = jnp.where(occ == o, eocc_ref[o], taken)
    negative = taken - picked
    erow[...] = negative[16:24]
    for i in range(16):
        ecol[i * 128:(i + 1) * 128] = jnp.broadcast_to(negative[i:i + 1], (128, 128)).T

    copies = []
    first = 0
    for i, size in enumerate(OUTER_ROWS):
        rows = slice(first, first + size)
        x = jnp.concatenate([dr_ref[0, rows], dr_ref[1, rows]], axis=1)
        h, l = split(x)
        acc = jnp.dot(h, ch[...], preferred_element_type=F32)
        acc += jnp.dot(l, ch[...], preferred_element_type=F32)
        acc += jnp.dot(h, cl[...], preferred_element_type=F32)
        e = ecol[rows]
        for n in range(8):
            lanes = slice(n * 128, (n + 1) * 128)
            obuf[rows, lanes] = acc[:, lanes] / (e + erow[n:n + 1])
        copies.append(pltpu.make_async_copy(obuf.at[rows], out_hbm.at[rows], sem.at[i]))
        copies[-1].start()
        first += size
    for c in copies:
        c.wait()


def local(amplitudes, factors, occ_index, vir_index, occ_energy, vir_energy):
    hbm = pl.BlockSpec(memory_space=pl.ANY)
    vmem = lambda *shape: pltpu.VMEM(shape, F32)
    dr, dc = pl.pallas_call(
        exchange_kernel,
        out_shape=(
            jax.ShapeDtypeStruct((2, 2, 8, 128, 128), F32),
            jax.ShapeDtypeStruct((2, 8, 128, 128), F32),
        ),
        in_specs=[hbm, pl.BlockSpec(memory_space=pltpu.HBM)],
        out_specs=(hbm, hbm),
        scratch_shapes=[
            vmem(2048, 1024),
            pltpu.VMEM((4, 2048, 256), BF16),
            pltpu.VMEM((4, 2048, 256), BF16),
            vmem(2, 4, 2, 16, 2048),
            pltpu.VMEM((256, 2048), BF16),
            vmem(2, 4, 2, 128, 128),
            vmem(2, 7, 128, 128),
            vmem(2, 128, 128),
            vmem(2, 128, 128),
            pltpu.SemaphoreType.DMA((len(NAMES),)),
            pltpu.SemaphoreType.DMA((len(NAMES),)),
            pltpu.SemaphoreType.DMA((8,)),
            pltpu.SemaphoreType.DMA((3,)),
            pltpu.SemaphoreType.DMA((2,)),
        ],
        compiler_params=pltpu.CompilerParams(
            collective_id=0, has_side_effects=True, vmem_limit_bytes=48 * 1024 * 1024),
        name="exchange",
    )(amplitudes, pltpu.with_memory_space_constraint(factors.T, pltpu.HBM))
    in_vmem = pl.BlockSpec(memory_space=pltpu.VMEM)
    return pl.pallas_call(
        outer_kernel,
        out_shape=jax.ShapeDtypeStruct((2048, 1024), F32),
        in_specs=[in_vmem] * 5 + [pl.BlockSpec(memory_space=pltpu.SMEM)],
        out_specs=hbm,
        scratch_shapes=[
            pltpu.VMEM((256, 1024), BF16),
            pltpu.VMEM((256, 1024), BF16),
            vmem(2048, 128),
            vmem(8, 128),
            vmem(2048, 1024),
            pltpu.SemaphoreType.DMA((len(OUTER_ROWS),)),
        ],
        compiler_params=pltpu.CompilerParams(vmem_limit_bytes=32 * 1024 * 1024),
        name="outer",
    )(
        dr.reshape(2, 2048, 128), dc, occ_index.reshape(128, 128), vir_index.reshape(128, 128),
        vir_energy.reshape(16, 128), occ_energy,
    )


def solution(mesh):
    return jax.shard_map(
        local,
        mesh=mesh,
        in_specs=(P("row", "col"), P("row", "col"), P(), P(), P(), P()),
        out_specs=P("row", "col"),
        check_vma=False,
    )
```
